32 devices in a mesh: groups: 2 (over y), tm: 4 (over z), space: 2 (over x), chan: 2 (over core).
Axes of the slice: x: 2, y: 2, z: 4, core: 2. Of those that a mesh axis runs over, the one named last changes fastest.
Arguments:
- activations: bfloat16 [256, 8, 16, 256], P(('groups', 'chan'), 'tm', 'space'), parts along dimension 0
- frame_clip: int32 [16], P(('groups', 'tm')), parts along dimension 0, may hold values from 0 to 3, as said below
- conv_weight: bfloat16 [3, 3, 3, 128, 128], replicated, may hold values from -0.109375 to 0.109375
- norm_gain: float32 [128], replicated, may hold values from 0.25 to 1.75
- norm_bias: float32 [128], replicated, may hold values from -3 to 3
- out_weight: bfloat16 [2, 2, 128, 32], replicated, may hold values from -0.25 to 0.25
- owner: int32 [4, 32, 1], P(('groups', 'space'), 'tm'), parts along dimension 0, may hold values from 0 to 3; in each aligned block of 8 rows (0 to 7, 8 to 15, ..., all dimensions but the last counted through in order) at most 4 rows name the same one
Outputs:
- owned: bfloat16 [4, 64, 32, 128], P(('groups', 'space'), 'tm', 'chan'), parts along dimension 0
The draws below stay inside these ranges and needn't reach their ends.
There are 2 independent parts, one for each index of `groups`. The reference program is written for one: setup_inputs(seed, part) draws one part's arguments, and reference() takes and returns one part's arrays. A program takes and returns all parts, laid end to end along the dimension named above; an argument that names none is the same for every part. Nothing has to cross between parts.
Inputs may be any that keep to these rules, and one draw needn't show every extreme that they name: `frame_clip`: clip numbers never fall along the frames; each clip has 1 to 4 frames and one has exactly 4. Among the 8 rows of one tm index (aligned blocks), no owner is named more than 4 times; some owner is named exactly 4 times in some block.
All inputs are finite; a program needn't handle non-finite values.
Results may differ from the reference program's by a relative error of at most 0.012.
Values may be sent and summed in bfloat16 or wider, within the bound.
A program may use at most 64 MiB of HBM per device.

```python
import math
import jax
import jax.numpy as jnp
import numpy as np
from jax import lax

CHANNELS = 128
GROUPS = 32
COLUMNS = 256
CLIPS = 4
MOMENTS = 32
HALF_ROWS = 4
HALF_COLS = 128
SEND_ROWS = 8
FRAMES = 8
HEIGHT = 16
LONGEST = 4
CAPACITY = 4
N_TM = 4
N_SPACE = 2


def draw_activations(key, part):
    key_base, key_rows, key_chan = jax.random.split(key, 3)
    frame_pos = jnp.arange(FRAMES, dtype=jnp.float32) / max(FRAMES - 1, 1)
    frame_scale = jnp.exp(jnp.log(3.0) * frame_pos)
    shape = (CHANNELS, FRAMES, HEIGHT, COLUMNS)
    base = jnp.clip(jax.random.normal(key_base, shape, jnp.float32), -6.0, 6.0)
    row_scale = jnp.exp(jax.random.uniform(key_rows, (1, FRAMES, HEIGHT, 1), jnp.float32, jnp.log(0.5), jnp.log(5.0)))
    chan_scale = jnp.exp(jax.random.uniform(key_chan, (CHANNELS, 1, 1, 1), jnp.float32, jnp.log(0.5), jnp.log(2.0)))
    return (base * row_scale * chan_scale * frame_scale[None, :, None, None]).astype(jnp.bfloat16)


def draw_frame_clip(key, part):
    key_cuts, key_place = jax.random.split(jax.random.fold_in(key, 7), 2)
    remain = FRAMES - LONGEST
    picked = jax.random.permutation(key_cuts, remain - 1)[:CLIPS - 2] + 1
    cuts = jnp.sort(picked).astype(jnp.int32)
    bounds = jnp.concatenate([jnp.zeros((1,), jnp.int32), cuts, jnp.full((1,), remain, jnp.int32)])
    others = bounds[1:] - bounds[:-1]
    place = jax.random.randint(key_place, (), 0, CLIPS, dtype=jnp.int32)
    index = jnp.arange(CLIPS, dtype=jnp.int32)
    other_index = jnp.clip(index - (index > place).astype(jnp.int32), 0, CLIPS - 2)
    lengths = jnp.where(index == place, LONGEST, others[other_index]).astype(jnp.int32)
    ends = jnp.cumsum(lengths).astype(jnp.int32)
    frames = jnp.arange(FRAMES, dtype=jnp.int32)
    return jnp.sum((frames[:, None] >= ends[None, :CLIPS - 1]).astype(jnp.int32), axis=1).astype(jnp.int32)


def shared_out(rng, own, number, rows, count, top, bound, slope):
    ranking = jax.random.permutation(rng, count)
    heavy_load, usual = load_shares(count, rows * top, bound, slope, True), load_shares(count, rows * top, bound, slope, False)
    places = jnp.arange(count)

    def named(sizes, turn):
        used = int((sizes > 0).sum())
        fixed = max(1, used // 4)
        shifted = fixed + (places - fixed + turn * (used - fixed)) % max(1, count - fixed)
        return jnp.zeros((count,), jnp.int32).at[ranking[jnp.where(places < fixed, places, shifted)]].set(jnp.asarray(sizes, jnp.int32))

    sizes = jnp.where(number % 4 == 0, named(heavy_load, number // 4), named(usual, number - number // 4 - 1))
    mixed = jax.random.permutation(jax.random.fold_in(own, 3), count)
    giver, receiver = mixed[0:count // 2 * 2:2], mixed[1:count // 2 * 2:2]
    margin = jnp.minimum(sizes[giver] - 1, bound - sizes[receiver]) // 2
    margin = jnp.where((giver == ranking[0]) | (receiver == ranking[0]) | (sizes[receiver] == 0), 0, jnp.maximum(margin, 0))
    shifted = jax.random.randint(jax.random.fold_in(own, 4), (count // 2,), 0, 1 << 20) % (margin + 1)
    sizes = sizes.at[giver].add(-shifted).at[receiver].add(shifted)
    items = jnp.searchsorted(jnp.cumsum(sizes), jnp.arange(rows * top), side="right").astype(jnp.int32)
    grid = items.reshape(top, rows).T
    grid = grid[jax.random.permutation(jax.random.fold_in(own, 1), rows)]
    turn = jax.random.randint(jax.random.fold_in(own, 2), (rows, 1), 0, top)
    return jnp.take_along_axis(grid, (jnp.arange(top)[None, :] + turn) % top, axis=1)


def load_shares(amount, total, reach, slope, full):
    loads = [(1 << 20) // math.isqrt(standing ** slope) + 1 for standing in range(1, amount + 1)]
    largest = reach if full else min(reach, max(-(-total // amount), total * loads[0] // sum(loads)))
    least = 1 if total - largest >= amount - 1 else 0
    given, rest = [largest] + [least] * (amount - 1), total - largest - least * (amount - 1)
    while rest > 0:
        movable = [i for i in range(1, amount) if given[i] < largest] or [i for i in range(1, amount) if given[i] < reach]
        whole, budget = sum([loads[i] for i in movable]), rest
        for i in movable:
            more = min(reach - given[i], max(1, budget * loads[i] // whole), rest)
            given[i] = given[i] + more
            rest = rest - more
    return np.array(given)


def noise(rng, shape, spread, bound, kind=jnp.bfloat16):
    drawn = jax.random.normal(rng, shape, jnp.float32) * spread
    return jnp.minimum(jnp.maximum(drawn, -bound), bound).astype(kind)


def setup_inputs(seed: int = 0, part: int = 0) -> dict:
    key_list = jax.random.split(jax.random.key(seed), 8)
    part_splits = jax.random.split(jax.random.fold_in(key_list[7], part), 8)
    activations = draw_activations(jax.random.fold_in(jax.random.fold_in(key_list[7], part), 71), part)
    frame_clip = draw_frame_clip(jax.random.fold_in(jax.random.fold_in(key_list[7], part), 71), part)
    conv_weight = noise(key_list[2], (3, 3, 3, CHANNELS, CHANNELS), (27 * CHANNELS) ** -0.5, 0.109375)
    norm_gain = jnp.clip(1.0 + 0.15 * jax.random.normal(key_list[3], (CHANNELS,), jnp.float32), 0.25, 1.75)
    norm_bias = noise(key_list[4], (CHANNELS,), 0.5, 3.0, jnp.float32)
    out_weight = noise(key_list[5], (2, 2, CHANNELS, MOMENTS), (4 * CHANNELS) ** -0.5, 0.25)
    owner_keys = jax.random.split(jax.random.fold_in(part_splits[6], 1), N_SPACE * (FRAMES * HALF_ROWS) // SEND_ROWS)
    owner_turns = jax.random.permutation(jax.random.fold_in(part_splits[6], 3), N_SPACE * (FRAMES * HALF_ROWS) // SEND_ROWS)
    owner = jax.vmap(lambda own, number: shared_out(jax.random.fold_in(part_splits[6], 2), own, number, SEND_ROWS, N_TM, 1, CAPACITY, 2))(owner_keys, owner_turns).reshape((N_SPACE, FRAMES * HALF_ROWS, 1))
    return dict(activations=activations, frame_clip=frame_clip, conv_weight=conv_weight, norm_gain=norm_gain, norm_bias=norm_bias, out_weight=out_weight, owner=owner)


def tap_list(clip_ids):
    frame_total = clip_ids.shape[0]
    position = jnp.arange(frame_total, dtype=jnp.int32)
    padded_ids = jnp.concatenate([jnp.full((2,), -1, jnp.int32), clip_ids])
    matches = [(padded_ids[m:m + frame_total] == clip_ids).astype(jnp.int32) for m in range(3)]
    result = []
    for k in range(3):
        number = matches[k]
        for m in range(k + 1, 3):
            number = number + matches[m]
        result.append(position + 1 - number)
    return result

def plane_conv(frames, kernel):
    return lax.conv_general_dilated(frames, kernel, (1, 1), ((1, 1), (1, 1)), dimension_numbers=('CNHW', 'HWIO', 'CNHW'), precision=lax.Precision.HIGHEST)

def reference(activations, frame_clip, conv_weight, norm_gain, norm_bias, out_weight, owner):
    source = activations.astype(jnp.float32)
    kernels = conv_weight.astype(jnp.float32)
    conv = jnp.zeros(activations.shape, jnp.float32)
    for k, tap_index in enumerate(tap_list(frame_clip)):
        conv = conv + plane_conv(jnp.take(source, tap_index, axis=1), kernels[k])
    conv = conv.astype(jnp.bfloat16).astype(jnp.float32)
    group_size = CHANNELS // GROUPS
    onehot = (frame_clip[:, None] == jnp.arange(CLIPS, dtype=jnp.int32)[None, :]).astype(jnp.float32)
    sums_one = lax.optimization_barrier(jnp.sum(conv, axis=(2, 3))).reshape(GROUPS, group_size, FRAMES).sum(1)
    sums_two = lax.optimization_barrier(jnp.sum(conv * conv, axis=(2, 3))).reshape(GROUPS, group_size, FRAMES).sum(1)
    sums_one = jnp.dot(sums_one, onehot, precision=lax.Precision.HIGHEST)
    sums_two = jnp.dot(sums_two, onehot, precision=lax.Precision.HIGHEST)
    counts = lax.optimization_barrier(jnp.sum(onehot, axis=0)) * (HEIGHT * COLUMNS * group_size)
    mean = sums_one / counts
    rstd = lax.rsqrt(sums_two / counts - mean * mean + 1e-06)
    mean_frame = jnp.repeat(jnp.dot(mean, onehot.T, precision=lax.Precision.HIGHEST), group_size, axis=0)
    rstd_frame = jnp.repeat(jnp.dot(rstd, onehot.T, precision=lax.Precision.HIGHEST), group_size, axis=0)
    scaled = (conv - mean_frame[:, :, None, None]) * rstd_frame[:, :, None, None]
    normed = jax.nn.silu(scaled * norm_gain[:, None, None, None] + norm_bias[:, None, None, None]).astype(jnp.bfloat16)
    patches = normed.astype(jnp.float32).reshape(CHANNELS, FRAMES, HEIGHT // 2, 2, HALF_COLS, 2)
    latent = jnp.einsum('cfrizj,ijco->ofrz', patches, out_weight.astype(jnp.float32), precision=lax.Precision.HIGHEST).astype(jnp.bfloat16)
    row_block = latent.reshape(MOMENTS, FRAMES, N_SPACE, HALF_ROWS, HALF_COLS)
    row_block = row_block.transpose(2, 1, 3, 0, 4).reshape(N_SPACE, FRAMES * HALF_ROWS, MOMENTS, HALF_COLS)
    blocks = owner[:, :, 0].reshape(N_SPACE, N_TM, SEND_ROWS)
    earlier = jnp.arange(SEND_ROWS)[None, :] < jnp.arange(SEND_ROWS)[:, None]
    equal = blocks[:, :, :, None] == blocks[:, :, None, :]
    order_rank = lax.optimization_barrier(jnp.sum((equal & earlier[None, None]).astype(jnp.int32), axis=3))
    target = blocks * (N_TM * CAPACITY) + jnp.arange(N_TM, dtype=jnp.int32)[None, :, None] * CAPACITY + order_rank
    target = target.reshape(N_SPACE, FRAMES * HALF_ROWS)
    owned = jnp.zeros((N_SPACE, N_TM * N_TM * CAPACITY, MOMENTS, HALF_COLS), jnp.bfloat16)
    owned = owned.at[jnp.arange(N_SPACE)[:, None], target].set(row_block)
    return owned
```

```python
import functools

import jax
import jax.numpy as jnp
from jax import lax
from jax.experimental import pallas as pl
from jax.experimental.pallas import tpu as pltpu
from jax.sharding import PartitionSpec as P

CHANNELS = 128
GROUPS = 32
GROUP_SIZE = CHANNELS // GROUPS
F32 = jnp.float32
BF16 = jnp.bfloat16
MESH = pl.DeviceIdType.MESH


def kernel(
    sizes, clip_hbm, owner_hbm, act_in, weight_in, gain_in, bias_in, out_weight_in, out,
    clip_in, owner_in, act_raw, act, weight, gain, bias, out_weight, meta_in,
    x, wt, conv, stat, stats, latent, arrived, meta, ids, sums,
    near_send, near_recv, zrow_send, zrow_recv, meta_send, meta_recv, stat_send, stat_recv,
    lat_send, lat_recv, extra_send, extra_recv, local_sem,
):
    n_tm, n_space, capacity, chunks = sizes
    frames_here, rows, half, columns = act.shape
    lanes = columns // 2
    total = n_tm * n_space * 2
    n_frames = n_tm * frames_here
    lat_rows = rows // 2
    step_rows = rows // chunks
    t = lax.axis_index("tm")
    s = lax.axis_index("space")
    c = lax.axis_index("chan")
    me = (t * n_space + s) * 2 + c
    first = t == 0
    piece_rows = lat_rows // 2
    reach = n_tm // 2
    has_main = jnp.logical_or(c == 1, t < n_tm - 1)

    def where_is(flat):
        return {"tm": flat // (2 * n_space), "space": (flat // 2) % n_space, "chan": flat % 2}

    fetches = [
        pltpu.make_async_copy(source, held, local_sem.at[1 + n])
        for n, (source, held) in enumerate((
            (act_in, act_raw), (weight_in, weight), (gain_in, gain), (bias_in, bias),
            (out_weight_in, out_weight),
            (clip_hbm, clip_in), (owner_hbm, owner_in),
        ))
    ]
    for fetch in fetches:
        fetch.start()
    stats[...] = jnp.zeros_like(stats)
    stat[...] = jnp.zeros_like(stat)

    barrier = pltpu.get_barrier_semaphore()

    @pl.loop(1, total)
    def _(step):
        pl.semaphore_signal(
            barrier, inc=1, device_id=where_is(lax.rem(me + step, total)), device_id_type=MESH
        )

    fetches[5].wait()
    fetches[6].wait()
    place = lax.broadcasted_iota(jnp.int32, (8, 128), 1)
    numbers = jnp.zeros((8, 128), jnp.int32)
    for n in range(frames_here):
        numbers = jnp.where(place == n, clip_in[0, n], numbers)
    for n in range(frames_here * lat_rows):
        numbers = jnp.where(place == frames_here + n, owner_in[0, n], numbers)
    meta_in[...] = numbers
    meta[t] = numbers
    fetches[0].wait()
    for f in range(frames_here):
        turned = jnp.transpose(act_raw[:, f], (1, 0, 2))
        act[f] = turned
        x[c + f, pl.ds(1, rows), c] = turned

    pl.semaphore_wait(barrier, total - 1)

    def remote(src, dst, send, recv, device):
        return pltpu.make_async_remote_copy(
            src_ref=src, dst_ref=dst, send_sem=send, recv_sem=recv, device_id=device,
            device_id_type=MESH,
        )

    def meta_copy(target):
        return remote(
            meta_in, meta.at[t], meta_send.at[target], meta_recv.at[t],
            {"tm": target, "space": s, "chan": c},
        )

    @pl.loop(1, n_tm)
    def _(step):
        meta_copy(lax.rem(t + step, n_tm)).start()

    up_ok, down_ok = t < n_tm - 1, t > 0
    t_up, t_down = jnp.minimum(t + 1, n_tm - 1), jnp.maximum(t - 1, 0)

    def zrow(up, piece):
        frame, slot, core, tt = (1, 0, 1, t_up) if up else (0, 2, 0, t_down)
        return remote(
            act.at[frame, pl.ds(piece * step_rows, step_rows)],
            x.at[slot, pl.ds(1 + piece * step_rows, step_rows), c],
            zrow_send.at[int(up), piece], zrow_recv.at[c, piece],
            {"tm": tt, "space": s, "chan": core},
        )

    def space_of(low):
        return jnp.maximum(s - 1, 0) if low else jnp.minimum(s + 1, n_space - 1)

    def edge(low, core):
        return remote(
            act.at[:, 0 if low else rows - 1],
            x.at[pl.ds(core, 2), rows + 1 if low else 0, c],
            near_send.at[int(low) * 2 + core], near_recv.at[int(low) * 2 + c],
            {"tm": t, "space": space_of(low), "chan": core},
        )

    def zedge(up, low):
        frame, slot, core, tt = (1, 0, 1, t_up) if up else (0, 2, 0, t_down)
        return remote(
            act.at[frame, 0 if low else rows - 1],
            x.at[slot, rows + 1 if low else 0, c],
            near_send.at[4 + int(low) * 2 + int(up)], near_recv.at[4 + int(low) * 2 + c],
            {"tm": tt, "space": space_of(low), "chan": core},
        )

    peer = remote(
        act, x.at[pl.ds(1 - c, 2), pl.ds(1, rows), c], near_send.at[8], near_recv.at[8],
        {"tm": t, "space": s, "chan": 1 - c},
    )
    low_ok, high_ok = s > 0, s < n_space - 1
    sides = ((True, low_ok), (False, high_ok))
    zs = ((True, up_ok), (False, down_ok))

    peer.start()
    for low, ok in sides:
        for up, z_ok in zs:
            @pl.when(jnp.logical_and(ok, z_ok))
            def _(low=low, up=up):
                zedge(up, low).start()
    for piece in range(chunks):
        for up, z_ok in zs:
            @pl.when(z_ok)
            def _(piece=piece, up=up):
                zrow(up, piece).start()
    for low, ok in sides:
        @pl.when(ok)
        def _(low=low):
            edge(low, 0).start()
            edge(low, 1).start()

    zero_row = jnp.zeros((3, 2, half, columns), BF16)

    @pl.when(s == 0)
    def _():
        x[:, 0] = zero_row

    @pl.when(s == n_space - 1)
    def _():
        x[:, rows + 1] = zero_row

    @pl.when(jnp.logical_and(first, c == 1))
    def _():
        x[0, pl.ds(1, rows)] = jnp.zeros((rows, 2, half, columns), BF16)

        @pl.when(s > 0)
        def _():
            x[0, 0] = zero_row[0]

        @pl.when(s < n_space - 1)
        def _():
            x[0, rows + 1] = zero_row[0]

    for fetch in fetches[1:5]:
        fetch.wait()
    for k in range(3):
        for i in range(3):
            for j in range(3):
                wt[k, pl.ds(j * 128, 128), pl.ds(i * 128, 128)] = weight[k, i, j].T
    gain_c = jnp.broadcast_to(gain[...], (128, 128)).T
    bias_c = jnp.broadcast_to(bias[...], (128, 128)).T * 0.5

    @pl.loop(1, n_tm)
    def _(step):
        source = lax.rem(t + step, n_tm)
        remote(
            meta_in, meta.at[source], meta_send.at[source], meta_recv.at[source],
            {"tm": source, "space": s, "chan": c},
        ).wait_recv()

    to_scalars = pltpu.make_async_copy(meta, ids, local_sem.at[0])
    to_scalars.start()
    to_scalars.wait()

    def clip_of(frame):
        frame = jnp.minimum(frame, n_frames - 1)
        return ids[frame // 2, 0, frame % 2]

    my_frame = 2 * t + 2 - c
    my_clip = clip_of(my_frame)
    older = jnp.logical_and(my_frame >= 2, clip_of(jnp.maximum(my_frame - 2, 0)) == my_clip)
    newer = clip_of(jnp.maximum(my_frame - 1, 0)) == my_clip

    peer.wait_recv()
    for low, ok in ((True, high_ok), (False, low_ok)):
        for core in range(2):
            @pl.when(ok)
            def _(low=low, core=core):
                remote(
                    act.at[:, 0], x.at[pl.ds(c, 2), rows + 1 if low else 0, core],
                    near_send.at[int(low) * 2 + core], near_recv.at[int(low) * 2 + core],
                    {"tm": t, "space": s, "chan": c},
                ).wait_recv()

    lane = lax.broadcasted_iota(jnp.int32, (CHANNELS, columns), 1)

    def conv_row(h, kept, taps):
        acc = None
        for k in range(3):
            term = jnp.dot(wt[k], taps[k](h), preferred_element_type=F32)
            acc = term if acc is None else acc + term
        left = jnp.where(lane == 0, 0.0, pltpu.roll(acc[0:128], 1, 1))
        right = jnp.where(lane == columns - 1, 0.0, pltpu.roll(acc[256:384], columns - 1, 1))
        value = (left + acc[128:256] + right).astype(BF16)
        conv[kept, h] = value
        value = value.astype(F32)
        a, b = value[:, :lanes], value[:, lanes:]
        sums[0] += a + b
        sums[1] += a * a + b * b

    def slab(slot):
        return lambda h: x[slot, pl.ds(h, 3)].reshape(3 * CHANNELS, columns)

    def sums_to(row):
        stat[pl.ds(row, 1), :] = jnp.sum(sums[0].T, axis=0, keepdims=True)
        stat[pl.ds(row + 1, 1), :] = jnp.sum(sums[1].T, axis=0, keepdims=True)

    @pl.when(first)
    def _():
        sums[...] = jnp.zeros_like(sums)

        @pl.loop(c * (rows // 2), (c + 1) * (rows // 2))
        def _(h):
            conv_row(h, 1, [slab(c)] * 3)

        sums_to(2)

    gets_z = jnp.logical_or(jnp.logical_and(c == 1, down_ok), jnp.logical_and(c == 0, up_ok))
    z_slot = 2 * (1 - c)

    def wait_zedge(low, ok):
        for core in range(2):
            @pl.when(jnp.logical_and(gets_z, ok))
            def _(core=core):
                remote(
                    act.at[0, 0], x.at[z_slot, rows + 1 if low else 0, core],
                    near_send.at[4 + int(low) * 2], near_recv.at[4 + int(low) * 2 + core],
                    {"tm": t, "space": s, "chan": c},
                ).wait_recv()

    def wait_zrow(piece):
        for core in range(2):
            @pl.when(gets_z)
            def _(core=core):
                remote(
                    act.at[0, pl.ds(piece * step_rows, step_rows)],
                    x.at[z_slot, pl.ds(1 + piece * step_rows, step_rows), core],
                    zrow_send.at[0, piece], zrow_recv.at[core, piece],
                    {"tm": t, "space": s, "chan": c},
                ).wait_recv()

    def tap_old(h):
        return jnp.where(older, slab(0)(h), tap_mid(h))

    def tap_mid(h):
        return jnp.where(newer, slab(1)(h), slab(2)(h))

    taps = [tap_old, tap_mid, slab(2)]
    wait_zedge(False, low_ok)
    wait_zedge(True, high_ok)

    @pl.when(has_main)
    def _():
        sums[...] = jnp.zeros_like(sums)

    for piece in range(chunks):
        wait_zrow(piece)
        begin = 0 if piece == 0 else piece * step_rows - 1
        end = rows if piece == chunks - 1 else (piece + 1) * step_rows - 1

        @pl.when(has_main)
        def _(begin=begin, end=end):
            @pl.loop(begin, end)
            def _(h):
                conv_row(h, 0, taps)

    @pl.when(has_main)
    def _():
        sums_to(0)

    def stat_copy(target):
        return remote(
            stat, stats.at[me], stat_send.at[target], stat_recv.at[me], where_is(target)
        )

    stats[me] = stat[...]

    def near(device):
        return jnp.abs(device // (2 * n_space) - t) <= reach

    @pl.loop(1, total)
    def _(step):
        target = lax.rem(me + step, total)

        @pl.when(near(target))
        def _():
            stat_copy(target).start()

    spread_row = lax.broadcasted_iota(jnp.int32, (columns, columns), 0)
    spread_col = lax.broadcasted_iota(jnp.int32, (columns, columns), 1)
    picked = jnp.where(spread_col < lanes, 2 * spread_col, 2 * (spread_col - lanes) + 1)
    spread = jnp.where(spread_row == picked, 1.0, 0.0).astype(BF16)

    @pl.loop(1, total)
    def _(step):
        source = lax.rem(me + step, total)

        @pl.when(near(source))
        def _():
            remote(
                stat, stats.at[source], stat_send.at[source], stat_recv.at[source],
                where_is(source),
            ).wait_recv()

    lane8 = lax.broadcasted_iota(jnp.int32, (8, 128), 1)

    def group_sum(v):
        v = v + jnp.where(lane8 % 2 == 0, pltpu.roll(v, 127, 1), pltpu.roll(v, 1, 1))
        return v + jnp.where(lane8 % 4 < 2, pltpu.roll(v, 126, 1), pltpu.roll(v, 2, 1))

    weights = jnp.concatenate([out_weight[q] for q in range(4)], axis=1)

    def moments_of(clip):
        def add_main(source, carry):
            frame = 2 * (source // (2 * n_space)) + 2 - source % 2
            same = jnp.logical_and(frame < n_frames, clip_of(frame) == clip)
            return carry + jnp.where(same, stats[source], 0.0)

        gathered = lax.fori_loop(0, total, add_main, jnp.zeros((8, 128), F32))
        zero_frame = jnp.zeros((8, 128), F32)
        for n in range(2 * n_space):
            zero_frame += stats[n]
        zero_frame = jnp.where(clip_of(0) == clip, zero_frame, 0.0)
        number = jnp.float32(0)
        for frame in range(n_frames):
            number += jnp.where(clip_of(frame) == clip, 1.0, 0.0)
        count = number * float(rows * n_space * columns * GROUP_SIZE)
        gathered = group_sum(gathered)
        zero_frame = group_sum(zero_frame)
        count = jnp.broadcast_to(count, (1, 128))
        mean = (gathered[0:1] + zero_frame[2:3]) / count
        var = (gathered[1:2] + zero_frame[3:4]) / count - mean * mean
        rstd = lax.rsqrt(var + 1e-6)
        mean_c = jnp.broadcast_to(mean, (128, 128)).T
        scale_c = jnp.broadcast_to(rstd, (128, 128)).T * gain_c * 0.5
        return mean_c, scale_c

    def finish(kept, piece, mean_c, scale_c):
        rows_in = []
        for q in range(2 * piece_rows):
            value = conv[kept, 2 * piece_rows * piece + q].astype(F32)
            pieces = []
            for u in range(2):
                v = (value[:, u * lanes:(u + 1) * lanes] - mean_c) * scale_c + bias_c
                pieces.append((v + v * jnp.tanh(v)).astype(BF16))
            rows_in.append(jnp.concatenate(pieces, axis=1))
        sorted_ = jnp.dot(
            jnp.concatenate(rows_in, axis=0), spread, preferred_element_type=F32
        ).astype(BF16)
        wide = jnp.concatenate(
            [
                jnp.concatenate(
                    [
                        sorted_[(2 * r + i) * 128:(2 * r + i + 1) * 128, j * lanes:(j + 1) * lanes]
                        for i in range(2) for j in range(2)
                    ],
                    axis=0,
                )
                for r in range(piece_rows)
            ],
            axis=1,
        )
        result = jnp.dot(weights, wide, preferred_element_type=F32).astype(BF16)
        for r in range(piece_rows):
            latent[kept, 0, piece * piece_rows + r] = result[0:16, r * lanes:(r + 1) * lanes]
            latent[kept, 1, piece * piece_rows + r] = result[16:32, r * lanes:(r + 1) * lanes]

    def lat_copy(kept, piece, frame, target, core, send, recv):
        span = pl.ds(piece * piece_rows, piece_rows)
        return remote(
            latent.at[kept, core, span], arrived.at[frame, span], send.at[target * 2 + core], recv,
            {"tm": target, "space": s, "chan": core},
        )

    here = t * 2 + c
    places = n_tm * 2

    def send_latent(kept, piece, frame, send, recv):
        span = pl.ds(piece * piece_rows, piece_rows)
        arrived[frame, span] = latent[kept, c, span]

        @pl.loop(1, places)
        def _(step):
            target = lax.rem(here + step, places)
            lat_copy(kept, piece, frame, target // 2, target % 2, send, recv).start()

    @pl.when(first)
    def _():
        finish(1, c, *moments_of(clip_of(0)))
        send_latent(1, c, 0, extra_send, extra_recv.at[c])

    @pl.when(has_main)
    def _():
        found = moments_of(my_clip)
        for piece in range(2):
            finish(0, piece, *found)
            send_latent(0, piece, my_frame, lat_send.at[piece], lat_recv.at[my_frame, piece])

    @pl.loop(1, n_frames)
    def _(frame):
        @pl.when(frame != my_frame)
        def _():
            for piece in range(2):
                lat_copy(
                    0, piece, frame, t, c, lat_send.at[piece], lat_recv.at[frame, piece]
                ).wait_recv()

    for piece in range(2):
        @pl.when(jnp.logical_not(jnp.logical_and(first, c == piece)))
        def _(piece=piece):
            lat_copy(0, piece, 0, t, c, lat_send.at[piece], extra_recv.at[piece]).wait_recv()

    @pl.loop(0, n_tm)
    def _(b):
        taken = jnp.int32(0)
        slots = []
        for n in range(2 * lat_rows):
            hit = ids[b, 0, frames_here + n] == t
            slots.append(jnp.where(hit, taken, -1))
            taken = taken + jnp.where(hit, 1, 0)
        for j in range(capacity):
            value = jnp.zeros((16, lanes), BF16)
            for n in range(2 * lat_rows):
                row = arrived[2 * b + n // lat_rows, n % lat_rows]
                value = jnp.where(slots[n] == j, row, value)
            out[0, b * capacity + j] = value

    @pl.loop(1, n_tm)
    def _(step):
        meta_copy(lax.rem(t + step, n_tm)).wait_send()

    peer.wait_send()
    for low, ok in sides:
        for up, z_ok in zs:
            @pl.when(jnp.logical_and(ok, z_ok))
            def _(low=low, up=up):
                zedge(up, low).wait_send()

        @pl.when(ok)
        def _(low=low):
            edge(low, 0).wait_send()
            edge(low, 1).wait_send()
    for piece in range(chunks):
        for up, z_ok in zs:
            @pl.when(z_ok)
            def _(piece=piece, up=up):
                zrow(up, piece).wait_send()

    @pl.loop(1, total)
    def _(step):
        target = lax.rem(me + step, total)

        @pl.when(near(target))
        def _():
            stat_copy(target).wait_send()

    def latents_left(kept, piece, frame, send, recv):
        @pl.loop(1, places)
        def _(step):
            target = lax.rem(here + step, places)
            lat_copy(kept, piece, frame, target // 2, target % 2, send, recv).wait_send()

    @pl.when(first)
    def _():
        latents_left(1, c, 0, extra_send, extra_recv.at[c])

    @pl.when(has_main)
    def _():
        for piece in range(2):
            latents_left(0, piece, my_frame, lat_send.at[piece], lat_recv.at[my_frame, piece])


def solution(mesh):
    n_tm, n_space = mesh.shape["tm"], mesh.shape["space"]
    total = n_tm * n_space * 2

    def shards(activations, frame_clip, conv_weight, norm_gain, norm_bias, out_weight, owner):
        half, frames_here, rows, columns = activations.shape
        lat_rows = rows // 2
        capacity = max(2, 2 * frames_here * lat_rows // n_tm)
        chunks = rows
        moments = out_weight.shape[-1]
        dma = pltpu.SemaphoreType.DMA
        return pl.pallas_call(
            functools.partial(kernel, (n_tm, n_space, capacity, chunks)),
            out_shape=jax.ShapeDtypeStruct(
                (1, n_tm * capacity, moments // 2, columns // 2), BF16
            ),
            in_specs=[pl.BlockSpec(memory_space=pltpu.HBM)] * 7,
            out_specs=pl.BlockSpec(memory_space=pltpu.VMEM),
            scratch_shapes=[
                pltpu.SMEM((1, frames_here), jnp.int32),
                pltpu.SMEM((1, frames_here * lat_rows), jnp.int32),
                pltpu.VMEM(activations.shape, BF16),
                pltpu.VMEM((frames_here, rows, half, columns), BF16),
                pltpu.VMEM(conv_weight.shape, BF16),
                pltpu.VMEM((1, CHANNELS), F32),
                pltpu.VMEM((1, CHANNELS), F32),
                pltpu.VMEM((4, moments, CHANNELS), BF16),
                pltpu.VMEM((8, 128), jnp.int32),
                pltpu.VMEM((3, rows + 2, 2, half, columns), BF16),
                pltpu.VMEM((3, 384, 384), BF16),
                pltpu.VMEM((2, rows, CHANNELS, columns), BF16),
                pltpu.VMEM((8, 128), F32),
                pltpu.VMEM((total, 8, 128), F32),
                pltpu.VMEM((2, 2, lat_rows, moments // 2, columns // 2), BF16),
                pltpu.VMEM((n_tm * frames_here, lat_rows, moments // 2, columns // 2), BF16),
                pltpu.VMEM((n_tm, 8, 128), jnp.int32),
                pltpu.SMEM((n_tm, 8, 128), jnp.int32),
                pltpu.VMEM((2, CHANNELS, columns // 2), F32),
                dma((9,)),
                dma((9,)),
                dma((2, chunks)),
                dma((2, chunks)),
                dma((n_tm,)),
                dma((n_tm,)),
                dma((total,)),
                dma((total,)),
                dma((2, 2 * n_tm)),
                dma((n_tm * frames_here, 2)),
                dma((2 * n_tm,)),
                dma((2,)),
                dma((8,)),
            ],
            compiler_params=pltpu.CompilerParams(
                collective_id=0, has_side_effects=True, vmem_limit_bytes=24 * 1024 * 1024
            ),
        )(*(
            pltpu.with_memory_space_constraint(operand, pltpu.HBM)
            for operand in (
                frame_clip.reshape(1, -1), owner.reshape(1, -1), activations, conv_weight,
                norm_gain.reshape(1, -1), norm_bias.reshape(1, -1),
                out_weight.transpose(0, 1, 3, 2).reshape(4, moments, CHANNELS),
            )
        ))

    placed = (
        P(("groups", "chan"), "tm", "space", None),
        P(("groups", "tm")),
        P(),
        P(),
        P(),
        P(),
        P(("groups", "space"), "tm", None),
    )
    return jax.shard_map(
        shards,
        mesh=mesh,
        in_specs=placed,
        out_specs=P(("groups", "space"), "tm", "chan", None),
        check_vma=False,
    )
```

```python
import functools

import jax
import jax.numpy as jnp
from jax import lax
from jax.experimental import pallas as pl
from jax.experimental.pallas import tpu as pltpu
from jax.sharding import PartitionSpec as P

CHANNELS = 128
GROUPS = 32
GROUP_SIZE = CHANNELS // GROUPS
F32 = jnp.float32
BF16 = jnp.bfloat16
MESH = pl.DeviceIdType.MESH


def kernel(
    sizes, clip_hbm, owner_hbm, act_in, weight_in, gain_in, bias_in, out_weight_in, out,
    clip_in, owner_in, act_raw, weight, gain, bias, out_weight, meta_in, near_meta, near_ids,
    x, wt, conv, stat, stats, ids, latent, arrived, sums,
    round_sem, z_send, z_recv, edge_send, edge_recv, fwd_send, fwd_recv, peer_send, peer_recv,
    meta_send, meta_recv, stat_send, stat_recv, lat_send, lat_recv, local_sem,
):
    n_tm, n_space, capacity = sizes
    half, frames_here, rows, columns = act_raw.shape
    lanes = columns // 2
    total = n_tm * n_space * 2
    n_frames = n_tm * frames_here
    lat_rows = rows // 2
    own_rows = frames_here * lat_rows
    piece_rows = lat_rows // 2
    half_rows = rows // 2
    t = lax.axis_index("tm")
    s = lax.axis_index("space")
    c = lax.axis_index("chan")
    me = (t * n_space + s) * 2 + c
    first = t == 0
    has_main = jnp.logical_or(c == 1, t < n_tm - 1)
    mirror = n_space == 2
    flip = s == 0 if mirror else False
    rounds = max(n_tm // 2 + n_space - 1, n_tm - 1) - 1

    def row_of(p):
        return jnp.where(flip, rows - 1 - p, p) if mirror else p

    fetches = [
        pltpu.make_async_copy(source, held, local_sem.at[n])
        for n, (source, held) in enumerate((
            (act_in, act_raw), (clip_hbm, clip_in), (owner_hbm, owner_in), (weight_in, weight),
            (gain_in, gain), (bias_in, bias), (out_weight_in, out_weight),
        ))
    ]
    for fetch in fetches:
        fetch.start()
    stats[...] = jnp.full(stats.shape, -1.0, F32)

    up_ok, down_ok = t < n_tm - 1, t > 0
    low_ok, high_ok = s > 0, s < n_space - 1
    t_up, t_down = jnp.minimum(t + 1, n_tm - 1), jnp.maximum(t - 1, 0)
    s_low, s_high = jnp.maximum(s - 1, 0), jnp.minimum(s + 1, n_space - 1)
    around = [(up_ok, t_up, s), (down_ok, t_down, s), (low_ok, t, s_low), (high_ok, t, s_high)]
    near_count = jnp.int32(1)
    for ok, _, _ in around:
        near_count = near_count + jnp.where(ok, 2, 0)

    def greet(semaphore):
        for ok, tt, ss in around:
            @pl.when(ok)
            def _(tt=tt, ss=ss):
                for core in range(2):
                    pl.semaphore_signal(
                        semaphore, inc=1, device_id={"tm": tt, "space": ss, "chan": core},
                        device_id_type=MESH,
                    )
        pl.semaphore_signal(
            semaphore, inc=1, device_id={"tm": t, "space": s, "chan": 1 - c}, device_id_type=MESH
        )

    barrier = pltpu.get_barrier_semaphore()
    greet(barrier)

    zero_row = jnp.zeros((3, 2, half, columns), BF16)

    @pl.when(s == 0)
    def _():
        x[:, 0] = zero_row

    @pl.when(s == n_space - 1)
    def _():
        x[:, rows + 1] = zero_row

    fetches[1].wait()
    fetches[2].wait()
    place = lax.broadcasted_iota(jnp.int32, (8, 128), 1)
    numbers = jnp.zeros((8, 128), jnp.int32)
    for n in range(frames_here):
        numbers = jnp.where(place == n, clip_in[0, n], numbers)
    meta_in[...] = numbers

    @pl.when(first)
    def _():
        near_meta[0] = numbers

    @pl.when(t == n_tm - 1)
    def _():
        near_meta[1] = numbers

    fetches[0].wait()
    for f in range(frames_here):
        x[c + f, pl.ds(1, rows), c] = jnp.transpose(act_raw[:, f], (1, 0, 2))

    pl.semaphore_wait(barrier, near_count)

    def remote(src, dst, send, recv, device):
        return pltpu.make_async_remote_copy(
            src_ref=src, dst_ref=dst, send_sem=send, recv_sem=recv, device_id=device,
            device_id_type=MESH,
        )

    def z_copy(up, p, count):
        frame, slot, core, tt = (1, 0, 1, t_up) if up else (0, 2, 0, t_down)
        begin = 1 + (jnp.where(flip, rows - p - count, p) if mirror else p)
        return remote(
            x.at[c + frame, pl.ds(begin, count), c], x.at[slot, pl.ds(begin, count), c],
            z_send.at[int(up)], z_recv.at[p], {"tm": tt, "space": s, "chan": core},
        )

    def meta_copy(up):
        return remote(
            meta_in, near_meta.at[0 if up else 1], meta_send.at[int(up)],
            meta_recv.at[0 if up else 1],
            {"tm": t_up if up else t_down, "space": s, "chan": c},
        )

    def edge(low, core):
        return remote(
            x.at[pl.ds(c, 2), 1 if low else rows, c],
            x.at[pl.ds(core, 2), rows + 1 if low else 0, c],
            edge_send.at[int(low)], edge_recv.at[int(low)],
            {"tm": t, "space": s_low if low else s_high, "chan": core},
        )

    z_slot = 2 * (1 - c)

    def forward(low):
        return remote(
            x.at[z_slot, 1 if low else rows], x.at[z_slot, rows + 1 if low else 0],
            fwd_send.at[int(low)], fwd_recv.at[int(low)],
            {"tm": t, "space": s_low if low else s_high, "chan": c},
        )

    peer = remote(
        x.at[pl.ds(c, 2), pl.ds(1, rows), c], x.at[pl.ds(1 - c, 2), pl.ds(1, rows), c],
        peer_send.at[0], peer_recv.at[0], {"tm": t, "space": s, "chan": 1 - c},
    )
    zs = ((True, up_ok), (False, down_ok))
    sides = ((True, low_ok), (False, high_ok))

    for p in range(2):
        for up, ok in zs:
            @pl.when(ok)
            def _(up=up, p=p):
                z_copy(up, p, 1).start()
    peer.start()
    for low, ok in sides:
        @pl.when(ok)
        def _(low=low):
            edge(low, 0).start()
            edge(low, 1).start()
    for up, ok in zs:
        @pl.when(ok)
        def _(up=up):
            meta_copy(up).start()
    for p in range(2, rows):
        for up, ok in zs:
            @pl.when(ok)
            def _(up=up, p=p):
                z_copy(up, p, 1).start()
    if rounds > 0:
        greet(round_sem.at[0])

    fetches[3].wait()
    for k in range(3):
        for i in range(3):
            for j in range(3):
                wt[k, pl.ds(j * 128, 128), pl.ds(i * 128, 128)] = weight[k, i, j].T
    for fetch in fetches[4:]:
        fetch.wait()

    for up, ok in zs:
        @pl.when(ok)
        def _(up=up):
            meta_copy(not up).wait_recv()
    to_scalars = pltpu.make_async_copy(near_meta, near_ids, local_sem.at[7])
    to_scalars.start()
    to_scalars.wait()

    my_clip = jnp.where(c == 1, clip_in[0, 1], near_ids[1, 0, 0])
    newer = jnp.where(c == 1, clip_in[0, 0], clip_in[0, 1]) == my_clip
    older = jnp.logical_and(
        jnp.logical_or(c == 0, t > 0),
        jnp.where(c == 1, near_ids[0, 0, 1], clip_in[0, 0]) == my_clip,
    )

    peer.wait_recv()
    if rounds > 0:
        pl.semaphore_wait(round_sem.at[0], near_count)

        @pl.loop(1, rounds)
        def _(r):
            greet(round_sem.at[lax.rem(r, 2)])

            @pl.when(r < rounds - 1)
            def _():
                pl.semaphore_wait(round_sem.at[lax.rem(r, 2)], near_count)

    lane = lax.broadcasted_iota(jnp.int32, (CHANNELS, columns), 1)

    def conv_row(h, kept, taps):
        acc = None
        for k in range(3):
            term = jnp.dot(wt[k], taps[k](h), preferred_element_type=F32)
            acc = term if acc is None else acc + term
        left = jnp.where(lane == 0, 0.0, pltpu.roll(acc[0:128], 1, 1))
        right = jnp.where(lane == columns - 1, 0.0, pltpu.roll(acc[256:384], columns - 1, 1))
        value = (left + acc[128:256] + right).astype(BF16)
        conv[kept, h] = value
        value = value.astype(F32)
        a, b = value[:, :lanes], value[:, lanes:]
        sums[0] += a + b
        sums[1] += a * a + b * b

    def slab(slot):
        return lambda h: x[slot, pl.ds(h, 3)].reshape(3 * CHANNELS, columns)

    def sums_to(row):
        stat[pl.ds(row, 1), :] = jnp.sum(sums[0].T, axis=0, keepdims=True)
        stat[pl.ds(row + 1, 1), :] = jnp.sum(sums[1].T, axis=0, keepdims=True)

    def wait_edges():
        for low, ok in ((True, high_ok), (False, low_ok)):
            @pl.when(ok)
            def _(low=low):
                there = x.at[pl.ds(c, 2), rows + 1 if low else 0]
                remote(
                    there, there, edge_send.at[int(low)], edge_recv.at[int(low)],
                    {"tm": t, "space": s, "chan": c},
                ).wait_recv()

    gets_z = jnp.logical_or(jnp.logical_and(c == 1, down_ok), jnp.logical_and(c == 0, up_ok))

    def wait_z(p):
        @pl.when(gets_z)
        def _():
            there = x.at[z_slot, pl.ds(1 + row_of(p), 1)]
            remote(
                there, there, z_send.at[0], z_recv.at[p], {"tm": t, "space": s, "chan": c}
            ).wait_recv()

    def start_forwards():
        for low, ok in sides:
            @pl.when(jnp.logical_and(gets_z, ok))
            def _(low=low):
                forward(low).start()

    def wait_forwards():
        for low, ok in ((True, high_ok), (False, low_ok)):
            @pl.when(jnp.logical_and(gets_z, ok))
            def _(low=low):
                forward(low).wait_recv()

    row8 = lax.broadcasted_iota(jnp.int32, (8, 128), 0)
    lane8 = lax.broadcasted_iota(jnp.int32, (8, 128), 1)
    facts = jnp.where(row8 == 2, jnp.where(has_main, my_clip, -1).astype(F32), -1.0)
    facts = jnp.where(
        jnp.logical_and(row8 == 5, first), clip_in[0, 0].astype(F32), facts
    )
    for n in range(own_rows):
        facts = jnp.where(
            jnp.logical_and(row8 == 6, lane8 == n), owner_in[0, n].astype(F32), facts
        )
    stat[...] = facts

    half_index = jnp.where(flip, c, 1 - c) if mirror else c

    if not mirror:
        wait_edges()

    @pl.when(first)
    def _():
        sums[...] = jnp.zeros_like(sums)

        @pl.loop(0, half_rows)
        def _(n):
            if mirror:
                @pl.when(jnp.logical_and(c == 1, n == half_rows - 1))
                def _():
                    wait_edges()
            p = half_rows - 1 - n + jnp.where(c == 0, half_rows, 0) if mirror else (
                n + c * half_rows
            )
            conv_row(row_of(p), 1, [slab(c)] * 3)

        sums_to(3)

    def tap_old(h):
        return jnp.where(older, slab(0)(h), tap_mid(h))

    def tap_mid(h):
        return jnp.where(newer, slab(1)(h), slab(2)(h))

    taps = [tap_old, tap_mid, slab(2)]
    border_step = rows - 4

    if mirror:
        wait_z(0)
        start_forwards()
        wait_z(1)
    else:
        for p in range(rows):
            wait_z(p)
        start_forwards()
        wait_forwards()

    sums[...] = jnp.zeros_like(sums)

    @pl.loop(0, rows)
    def _(n):
        if mirror:
            @pl.when(n < border_step)
            def _():
                wait_z(n + 2)

            @pl.when(n == border_step)
            def _():
                @pl.when(jnp.logical_not(jnp.logical_and(first, c == 1)))
                def _():
                    wait_edges()
                wait_forwards()

            @pl.when(jnp.logical_and(n > border_step, n < rows - 1))
            def _():
                wait_z(n + 1)

            p = jnp.where(n < border_step, n + 1, jnp.where(n == border_step, 0, n))
        else:
            p = n

        @pl.when(has_main)
        def _():
            conv_row(row_of(p), 0, taps)

    @pl.when(has_main)
    def _():
        sums_to(0)

    if rounds > 1:
        pl.semaphore_wait(round_sem.at[(rounds - 1) % 2], near_count)

    stats[me] = stat[...]

    def needs(tt, ss, core):
        apart = jnp.abs(2 * (tt - t) + c - core) <= n_tm - 1
        return jnp.logical_or(apart, jnp.logical_and(ss == s, core == c))

    def stat_copy(tt, ss, core):
        target = (tt * n_space + ss) * 2 + core
        return remote(
            stat, stats.at[me], stat_send.at[target], stat_recv.at[me],
            {"tm": tt, "space": ss, "chan": core},
        )

    def stat_from(tt, ss, core):
        source = (tt * n_space + ss) * 2 + core
        return remote(
            stat, stats.at[source], stat_send.at[source], stat_recv.at[source],
            {"tm": tt, "space": ss, "chan": core},
        )

    def each_stat(act):
        @pl.loop(0, n_tm)
        def _(step):
            far = n_tm - 1 - step
            for up in (True, False):
                tt = t + far if up else t - far
                ok = jnp.logical_and(tt < n_tm, tt >= 0)
                if not up:
                    ok = jnp.logical_and(ok, far > 0)
                for ss in range(n_space):
                    for core in range(2):
                        use = jnp.logical_and(ok, needs(tt, ss, core))
                        other = (tt * n_space + ss) * 2 + core != me

                        @pl.when(jnp.logical_and(use, other))
                        def _(tt=tt, ss=ss, core=core):
                            act(tt, ss, core)

    each_stat(lambda tt, ss, core: stat_copy(tt, ss, core).start())

    spread_row = lax.broadcasted_iota(jnp.int32, (columns, lanes), 0)
    spread_col = lax.broadcasted_iota(jnp.int32, (columns, lanes), 1)
    spread = jnp.where(spread_row == 2 * spread_col, 1.0, 0.0).astype(BF16)
    weights = jnp.concatenate(
        [
            jnp.concatenate([out_weight[2 * i + j] for i in range(2)], axis=1)
            for j in range(2)
        ],
        axis=0,
    )

    each_stat(lambda tt, ss, core: stat_from(tt, ss, core).wait_recv())

    owners = [
        pltpu.make_async_copy(stats.at[(b * n_space + s) * 2 + c], ids.at[b], local_sem.at[8])
        for b in range(n_tm)
    ]
    for copy in owners:
        copy.start()

    sizes_row = jnp.where(
        row8 == 2, float(rows * columns), float(half_rows * columns)
    )
    is_size = jnp.logical_or(row8 == 2, row8 == 5)

    def add_source(source, carry, clip):
        value = stats[source]
        key = jnp.where(row8 < 3, value[2:3], value[5:6])
        value = jnp.where(is_size, sizes_row, value)
        return carry + jnp.where(key == clip, value, 0.0)

    def moments_of(clip):
        clip = clip.astype(F32)
        found = jnp.zeros((8, 128), F32)
        if total <= 32:
            for source in range(total):
                found = add_source(source, found, clip)
        else:
            found = lax.fori_loop(
                0, total, lambda source, carry: add_source(source, carry, clip), found
            )
        found = found + pltpu.roll(found, 5, 0)
        found = found + jnp.where(
            lane8 % 2 == 0, pltpu.roll(found, 127, 1), pltpu.roll(found, 1, 1)
        )
        found = found + jnp.where(
            lane8 % 4 < 2, pltpu.roll(found, 126, 1), pltpu.roll(found, 2, 1)
        )
        count = found[2:3]
        mean = found[0:1] / count
        var = found[1:2] / count - mean * mean
        scale = lax.rsqrt(var + 1e-6) * gain[...] * 0.5
        shift = bias[...] * 0.5 - mean * scale
        return jnp.broadcast_to(scale, (128, 128)).T, jnp.broadcast_to(shift, (128, 128)).T

    def finish(kept, begin, scale_c, shift_c):
        packed = []
        for r in range(piece_rows):
            pair = []
            for i in range(2):
                value = conv[kept, 2 * (begin + r) + i].astype(F32)
                pieces = []
                for u in range(2):
                    v = value[:, u * lanes:(u + 1) * lanes] * scale_c + shift_c
                    pieces.append((v + v * jnp.tanh(v)).astype(BF16))
                pair.append(jnp.concatenate(pieces, axis=1))
            both = jnp.dot(
                weights, jnp.concatenate(pair, axis=0), preferred_element_type=F32
            )
            packed.append((both[0:32] + pltpu.roll(both[32:64], columns - 1, 1)).astype(BF16))
        result = jnp.dot(
            jnp.concatenate(packed, axis=0), spread, preferred_element_type=F32
        ).astype(BF16)
        for r in range(piece_rows):
            for core in range(2):
                latent[kept, core, begin + r] = result[r * 32 + core * 16:r * 32 + core * 16 + 16]

    def send_latent(kept, begin, frame):
        span = pl.ds(frame * lat_rows + begin, piece_rows)
        arrived[span] = latent[kept, c, pl.ds(begin, piece_rows)]

        @pl.loop(0, n_tm)
        def _(step):
            far = n_tm - 1 - step
            for up in (True, False):
                tt = t + far if up else t - far
                ok = jnp.logical_and(tt < n_tm, tt >= 0)
                if not up:
                    ok = jnp.logical_and(ok, far > 0)
                for core in range(2):
                    other = jnp.logical_or(tt != t, core != c)

                    @pl.when(jnp.logical_and(ok, other))
                    def _(tt=tt, core=core):
                        remote(
                            latent.at[kept, core, pl.ds(begin, piece_rows)], arrived.at[span],
                            lat_send.at[kept], lat_recv.at[0],
                            {"tm": tt, "space": s, "chan": core},
                        ).start()

    my_frame = 2 * t + 2 - c

    @pl.when(first)
    def _():
        finish(1, half_index * piece_rows, *moments_of(clip_in[0, 0]))
        send_latent(1, half_index * piece_rows, 0)

    @pl.when(has_main)
    def _():
        found = moments_of(my_clip)
        for piece in range(2):
            finish(0, piece * piece_rows, *found)
            send_latent(0, piece * piece_rows, my_frame)

    pltpu.make_async_copy(stats.at[pl.ds(0, n_tm)], ids, local_sem.at[8]).wait()

    def arrived_wait(count):
        span = arrived.at[pl.ds(0, count)]
        remote(
            span, span, lat_send.at[0], lat_recv.at[0], {"tm": t, "space": s, "chan": c}
        ).wait_recv()

    every = n_frames * lat_rows

    @pl.when(first)
    def _():
        arrived_wait(every - lat_rows - piece_rows)

    @pl.when(jnp.logical_and(has_main, t > 0))
    def _():
        arrived_wait(every - lat_rows)

    @pl.when(jnp.logical_not(has_main))
    def _():
        arrived_wait(every)

    here = t.astype(F32)

    @pl.loop(0, n_tm)
    def _(b):
        taken = jnp.int32(0)
        slots = []
        for n in range(own_rows):
            hit = ids[b, 6, n] == here
            slots.append(jnp.where(hit, taken, -1))
            taken = taken + jnp.where(hit, 1, 0)
        for j in range(capacity):
            value = jnp.zeros((16, lanes), BF16)
            for n in range(own_rows):
                value = jnp.where(slots[n] == j, arrived[b * own_rows + n], value)
            out[0, b * capacity + j] = value

    peer.wait_send()
    for up, ok in zs:
        @pl.when(ok)
        def _(up=up):
            z_copy(up, 0, rows).wait_send()
            meta_copy(up).wait_send()
    for low, ok in sides:
        @pl.when(ok)
        def _(low=low):
            there = x.at[pl.ds(0, 2), 0]
            remote(
                there, there, edge_send.at[int(low)], edge_recv.at[int(low)],
                {"tm": t, "space": s, "chan": c},
            ).wait_send()

            @pl.when(gets_z)
            def _():
                forward(low).wait_send()

    each_stat(lambda tt, ss, core: stat_copy(tt, ss, core).wait_send())

    def latents_left(kept, count):
        span = arrived.at[pl.ds(0, count)]
        remote(
            span, span, lat_send.at[kept], lat_recv.at[0], {"tm": t, "space": s, "chan": c}
        ).wait_send()

    @pl.when(first)
    def _():
        latents_left(1, (2 * n_tm - 1) * piece_rows)

    @pl.when(has_main)
    def _():
        latents_left(0, (2 * n_tm - 1) * lat_rows)


def solution(mesh):
    n_tm, n_space = mesh.shape["tm"], mesh.shape["space"]
    total = n_tm * n_space * 2

    def shards(activations, frame_clip, conv_weight, norm_gain, norm_bias, out_weight, owner):
        half, frames_here, rows, columns = activations.shape
        lat_rows = rows // 2
        capacity = max(2, 2 * frames_here * lat_rows // n_tm)
        moments = out_weight.shape[-1]
        dma = pltpu.SemaphoreType.DMA
        return pl.pallas_call(
            functools.partial(kernel, (n_tm, n_space, capacity)),
            out_shape=jax.ShapeDtypeStruct(
                (1, n_tm * capacity, moments // 2, columns // 2), BF16
            ),
            in_specs=[pl.BlockSpec(memory_space=pltpu.HBM)] * 7,
            out_specs=pl.BlockSpec(memory_space=pltpu.VMEM),
            scratch_shapes=[
                pltpu.SMEM((1, frames_here), jnp.int32),
                pltpu.SMEM((1, frames_here * lat_rows), jnp.int32),
                pltpu.VMEM(activations.shape, BF16),
                pltpu.VMEM(conv_weight.shape, BF16),
                pltpu.VMEM((1, CHANNELS), F32),
                pltpu.VMEM((1, CHANNELS), F32),
                pltpu.VMEM((4, moments, CHANNELS), BF16),
                pltpu.VMEM((8, 128), jnp.int32),
                pltpu.VMEM((2, 8, 128), jnp.int32),
                pltpu.SMEM((2, 8, 128), jnp.int32),
                pltpu.VMEM((3, rows + 2, 2, half, columns), BF16),
                pltpu.VMEM((3, 384, 384), BF16),
                pltpu.VMEM((2, rows, CHANNELS, columns), BF16),
                pltpu.VMEM((8, 128), F32),
                pltpu.VMEM((total, 8, 128), F32),
                pltpu.SMEM((n_tm, 8, 128), F32),
                pltpu.VMEM((2, 2, lat_rows, moments // 2, columns // 2), BF16),
                pltpu.VMEM((n_tm * frames_here * lat_rows, moments // 2, columns // 2), BF16),
                pltpu.VMEM((2, CHANNELS, columns // 2), F32),
                pltpu.SemaphoreType.REGULAR((2,)),
                dma((2,)),
                dma((rows,)),
                dma((2,)),
                dma((2,)),
                dma((2,)),
                dma((2,)),
                dma((1,)),
                dma((1,)),
                dma((2,)),
                dma((2,)),
                dma((total,)),
                dma((total,)),
                dma((2,)),
                dma((1,)),
                dma((9,)),
            ],
            compiler_params=pltpu.CompilerParams(
                collective_id=0, has_side_effects=True, vmem_limit_bytes=24 * 1024 * 1024
            ),
        )(*(
            pltpu.with_memory_space_constraint(operand, pltpu.HBM)
            for operand in (
                frame_clip.reshape(1, -1), owner.reshape(1, -1), activations, conv_weight,
                norm_gain.reshape(1, -1), norm_bias.reshape(1, -1),
                out_weight.transpose(0, 1, 3, 2).reshape(4, moments, CHANNELS),
            )
        ))

    placed = (
        P(("groups", "chan"), "tm", "space", None),
        P(("groups", "tm")),
        P(),
        P(),
        P(),
        P(),
        P(("groups", "space"), "tm", None),
    )
    return jax.shard_map(
        shards,
        mesh=mesh,
        in_specs=placed,
        out_specs=P(("groups", "space"), "tm", "chan", None),
        check_vma=False,
    )
```

```python
import functools

import jax
import jax.numpy as jnp
from jax import lax
from jax.experimental import pallas as pl
from jax.experimental.pallas import tpu as pltpu
from jax.sharding import PartitionSpec as P

CHANNELS = 128
GROUPS = 32
GROUP_SIZE = CHANNELS // GROUPS
F32 = jnp.float32
BF16 = jnp.bfloat16
MESH = pl.DeviceIdType.MESH


def kernel(
    sizes, clip_hbm, owner_hbm, act_in, weight_in, gain_in, bias_in, out_weight_in, out,
    clip_in, owner_in, act_raw, weight, gain, bias, out_weight, meta_in, near_meta, near_ids,
    x, wt, conv, stat, stats, ids, latent, arrived, sums,
    round_sem, z_send, z_recv, edge_send, edge_recv, fwd_send, fwd_recv, peer_send, peer_recv,
    meta_send, meta_recv, stat_send, stat_recv, lat_send, lat_recv, local_sem,
):
    n_tm, n_space, capacity = sizes
    half, frames_here, rows, columns = act_raw.shape
    lanes = columns // 2
    total = n_tm * n_space * 2
    n_frames = n_tm * frames_here
    lat_rows = rows // 2
    own_rows = frames_here * lat_rows
    piece_rows = lat_rows // 2
    half_rows = rows // 2
    t = lax.axis_index("tm")
    s = lax.axis_index("space")
    c = lax.axis_index("chan")
    me = (t * n_space + s) * 2 + c
    first = t == 0
    has_main = jnp.logical_or(c == 1, t < n_tm - 1)
    mirror = n_space == 2
    flip = s == 0 if mirror else False
    window = 4
    rounds = max(n_tm // 2 + n_space - 1, n_tm - 1) - 1

    def row_of(p):
        return jnp.where(flip, rows - 1 - p, p) if mirror else p

    fetches = [
        pltpu.make_async_copy(source, held, local_sem.at[n])
        for n, (source, held) in enumerate((
            (act_in, act_raw), (clip_hbm, clip_in), (owner_hbm, owner_in), (weight_in, weight),
            (gain_in, gain), (bias_in, bias), (out_weight_in, out_weight),
        ))
    ]
    for fetch in fetches:
        fetch.start()
    stats[...] = jnp.full(stats.shape, -1.0, F32)

    up_ok, down_ok = t < n_tm - 1, t > 0
    low_ok, high_ok = s > 0, s < n_space - 1
    t_up, t_down = jnp.minimum(t + 1, n_tm - 1), jnp.maximum(t - 1, 0)
    s_low, s_high = jnp.maximum(s - 1, 0), jnp.minimum(s + 1, n_space - 1)
    around = [(up_ok, t_up, s), (down_ok, t_down, s), (low_ok, t, s_low), (high_ok, t, s_high)]
    near_count = jnp.int32(1)
    for ok, _, _ in around:
        near_count = near_count + jnp.where(ok, 2, 0)

    def greet(semaphore):
        for ok, tt, ss in around:
            @pl.when(ok)
            def _(tt=tt, ss=ss):
                for core in range(2):
                    pl.semaphore_signal(
                        semaphore, inc=1, device_id={"tm": tt, "space": ss, "chan": core},
                        device_id_type=MESH,
                    )
        pl.semaphore_signal(
            semaphore, inc=1, device_id={"tm": t, "space": s, "chan": 1 - c}, device_id_type=MESH
        )

    barrier = pltpu.get_barrier_semaphore()
    greet(barrier)

    zero_row = jnp.zeros((3, 2, half, columns), BF16)

    @pl.when(s == 0)
    def _():
        x[:, 0] = zero_row

    @pl.when(s == n_space - 1)
    def _():
        x[:, rows + 1] = zero_row

    fetches[1].wait()
    fetches[2].wait()
    place = lax.broadcasted_iota(jnp.int32, (8, 128), 1)
    numbers = jnp.zeros((8, 128), jnp.int32)
    for n in range(frames_here):
        numbers = jnp.where(place == n, clip_in[0, n], numbers)
    meta_in[...] = numbers

    @pl.when(first)
    def _():
        near_meta[0] = numbers

    @pl.when(t == n_tm - 1)
    def _():
        near_meta[1] = numbers

    fetches[0].wait()
    for f in range(frames_here):
        x[c + f, pl.ds(1, rows), c] = jnp.transpose(act_raw[:, f], (1, 0, 2))

    pl.semaphore_wait(barrier, near_count)

    def remote(src, dst, send, recv, device):
        return pltpu.make_async_remote_copy(
            src_ref=src, dst_ref=dst, send_sem=send, recv_sem=recv, device_id=device,
            device_id_type=MESH,
        )

    def z_copy(up, p, count):
        frame, slot, core, tt = (1, 0, 1, t_up) if up else (0, 2, 0, t_down)
        begin = 1 + (jnp.where(flip, rows - p - count, p) if mirror else p)
        return remote(
            x.at[c + frame, pl.ds(begin, count), c], x.at[slot, pl.ds(begin, count), c],
            z_send.at[int(up), p % window], z_recv.at[p], {"tm": tt, "space": s, "chan": core},
        )

    def meta_copy(up):
        return remote(
            meta_in, near_meta.at[0 if up else 1], meta_send.at[int(up)],
            meta_recv.at[0 if up else 1],
            {"tm": t_up if up else t_down, "space": s, "chan": c},
        )

    def edge(low, core):
        return remote(
            x.at[pl.ds(c, 2), 1 if low else rows, c],
            x.at[pl.ds(core, 2), rows + 1 if low else 0, c],
            edge_send.at[int(low)], edge_recv.at[int(low)],
            {"tm": t, "space": s_low if low else s_high, "chan": core},
        )

    z_slot = 2 * (1 - c)

    def forward(low):
        return remote(
            x.at[z_slot, 1 if low else rows], x.at[z_slot, rows + 1 if low else 0],
            fwd_send.at[int(low)], fwd_recv.at[int(low)],
            {"tm": t, "space": s_low if low else s_high, "chan": c},
        )

    peer = remote(
        x.at[pl.ds(c, 2), pl.ds(1, rows), c], x.at[pl.ds(1 - c, 2), pl.ds(1, rows), c],
        peer_send.at[0], peer_recv.at[0], {"tm": t, "space": s, "chan": 1 - c},
    )
    zs = ((True, up_ok), (False, down_ok))
    sides = ((True, low_ok), (False, high_ok))

    def start_z(p):
        for up, ok in zs:
            @pl.when(ok)
            def _(up=up):
                z_copy(up, p, 1).start()

    def start_edges():
        for low, ok in sides:
            @pl.when(ok)
            def _(low=low):
                edge(low, 0).start()
                edge(low, 1).start()

    def start_meta():
        for up, ok in zs:
            @pl.when(ok)
            def _(up=up):
                meta_copy(up).start()

    start_meta()
    peer.start()
    start_z(0)
    start_z(1)
    start_z(2)
    start_z(3)
    start_edges()

    def advance(p):
        if p + window < rows:
            for up, ok in zs:
                @pl.when(ok)
                def _(up=up):
                    z_copy(up, p, 1).wait_send()
                    z_copy(up, p + window, 1).start()

    if rounds > 0:
        greet(round_sem.at[0])

    fetches[3].wait()
    for k in range(3):
        for i in range(3):
            for j in range(3):
                wt[pl.ds(j * 128, 128), pl.ds((3 * k + i) * 128, 128)] = weight[k, i, j].T
    advance(0)
    for fetch in fetches[4:]:
        fetch.wait()

    for up, ok in zs:
        @pl.when(ok)
        def _(up=up):
            meta_copy(not up).wait_recv()
    to_scalars = pltpu.make_async_copy(near_meta, near_ids, local_sem.at[7])
    to_scalars.start()
    to_scalars.wait()

    my_clip = jnp.where(c == 1, clip_in[0, 1], near_ids[1, 0, 0])
    newer = jnp.where(c == 1, clip_in[0, 0], clip_in[0, 1]) == my_clip
    older = jnp.logical_and(
        jnp.logical_or(c == 0, t > 0),
        jnp.where(c == 1, near_ids[0, 0, 1], clip_in[0, 0]) == my_clip,
    )

    peer.wait_recv()
    advance(1)
    if rounds > 0:
        pl.semaphore_wait(round_sem.at[0], near_count)

        @pl.loop(1, rounds)
        def _(r):
            greet(round_sem.at[lax.rem(r, 2)])

            @pl.when(r < rounds - 1)
            def _():
                pl.semaphore_wait(round_sem.at[lax.rem(r, 2)], near_count)

    lane = lax.broadcasted_iota(jnp.int32, (CHANNELS, columns), 1)

    def conv_row(h, kept, taps):
        acc = jnp.dot(
            wt[...], jnp.concatenate([tap(h) for tap in taps], axis=0),
            preferred_element_type=F32,
        )
        left = jnp.where(lane == 0, 0.0, pltpu.roll(acc[0:128], 1, 1))
        right = jnp.where(lane == columns - 1, 0.0, pltpu.roll(acc[256:384], columns - 1, 1))
        value = (left + acc[128:256] + right).astype(BF16)
        conv[kept, h] = value
        value = value.astype(F32)
        a, b = value[:, :lanes], value[:, lanes:]
        return a + b, a * a + b * b

    def conv_pair(h, later, kept, taps):
        one, two = conv_row(h, kept, taps), conv_row(later, kept, taps)
        sums[0] += one[0] + two[0]
        sums[1] += one[1] + two[1]

    def slab(slot):
        return lambda h: x[slot, pl.ds(h, 3)].reshape(3 * CHANNELS, columns)

    def sums_to(row):
        stat[pl.ds(row, 1), :] = jnp.sum(sums[0].T, axis=0, keepdims=True)
        stat[pl.ds(row + 1, 1), :] = jnp.sum(sums[1].T, axis=0, keepdims=True)

    def wait_edges():
        for low, ok in ((True, high_ok), (False, low_ok)):
            @pl.when(ok)
            def _(low=low):
                there = x.at[pl.ds(c, 2), rows + 1 if low else 0]
                remote(
                    there, there, edge_send.at[int(low)], edge_recv.at[int(low)],
                    {"tm": t, "space": s, "chan": c},
                ).wait_recv()

    gets_z = jnp.logical_or(jnp.logical_and(c == 1, down_ok), jnp.logical_and(c == 0, up_ok))

    def wait_z(p):
        @pl.when(gets_z)
        def _():
            there = x.at[z_slot, pl.ds(1 + row_of(p), 1)]
            remote(
                there, there, z_send.at[0], z_recv.at[p], {"tm": t, "space": s, "chan": c}
            ).wait_recv()

    def start_forwards():
        for low, ok in sides:
            @pl.when(jnp.logical_and(gets_z, ok))
            def _(low=low):
                forward(low).start()

    def wait_forwards():
        for low, ok in ((True, high_ok), (False, low_ok)):
            @pl.when(jnp.logical_and(gets_z, ok))
            def _(low=low):
                forward(low).wait_recv()

    row8 = lax.broadcasted_iota(jnp.int32, (8, 128), 0)
    lane8 = lax.broadcasted_iota(jnp.int32, (8, 128), 1)
    facts = jnp.where(row8 == 2, jnp.where(has_main, my_clip, -1).astype(F32), -1.0)
    facts = jnp.where(
        jnp.logical_and(row8 == 5, first), clip_in[0, 0].astype(F32), facts
    )
    for n in range(own_rows):
        facts = jnp.where(
            jnp.logical_and(row8 == 6, lane8 == n), owner_in[0, n].astype(F32), facts
        )
    stat[...] = facts

    half_index = jnp.where(flip, c, 1 - c) if mirror else c

    if not mirror:
        wait_edges()

    @pl.when(first)
    def _():
        sums[...] = jnp.zeros_like(sums)

        @pl.loop(0, half_rows // 2)
        def _(n):
            if mirror:
                @pl.when(n == half_rows // 2 - 1)
                def _():
                    for p in range(2, rows):
                        advance(p)

                    @pl.when(c == 1)
                    def _():
                        wait_edges()
            p = half_rows - 1 - 2 * n + jnp.where(c == 0, half_rows, 0) if mirror else (
                2 * n + 1 + c * half_rows
            )
            conv_pair(row_of(p), row_of(p - 1), 1, [slab(c)] * 3)

        sums_to(3)

    def tap_old(h):
        return jnp.where(older, slab(0)(h), tap_mid(h))

    def tap_mid(h):
        return jnp.where(newer, slab(1)(h), slab(2)(h))

    taps = [tap_old, tap_mid, slab(2)]
    steps = rows // 2

    @pl.when(jnp.logical_not(first) if mirror else True)
    def _():
        for p in range(2, rows):
            advance(p)

    if mirror:
        wait_z(0)
        start_forwards()
        wait_z(1)
    else:
        for p in range(rows):
            wait_z(p)
        start_forwards()
        wait_forwards()

    sums[...] = jnp.zeros_like(sums)

    @pl.loop(0, steps)
    def _(n):
        if mirror:
            @pl.when(n < steps - 2)
            def _():
                wait_z(2 * n + 2)
                wait_z(2 * n + 3)

            @pl.when(n == steps - 2)
            def _():
                wait_z(rows - 2)

                @pl.when(jnp.logical_not(jnp.logical_and(first, c == 1)))
                def _():
                    wait_edges()
                wait_forwards()

            @pl.when(n == steps - 1)
            def _():
                wait_z(rows - 1)

            p = jnp.where(n == steps - 1, rows - 2, 2 * n + 1)
            later = jnp.where(n < steps - 2, 2 * n + 2, jnp.where(n == steps - 2, 0, rows - 1))
        else:
            p, later = 2 * n, 2 * n + 1

        @pl.when(has_main)
        def _():
            conv_pair(row_of(p), row_of(later), 0, taps)

    @pl.when(has_main)
    def _():
        sums_to(0)

    if rounds > 1:
        pl.semaphore_wait(round_sem.at[(rounds - 1) % 2], near_count)

    stats[me] = stat[...]

    def needs(tt, ss, core):
        apart = jnp.abs(2 * (tt - t) + c - core) <= n_tm - 1
        return jnp.logical_or(apart, jnp.logical_and(ss == s, core == c))

    def stat_copy(tt, ss, core):
        target = (tt * n_space + ss) * 2 + core
        return remote(
            stat, stats.at[me], stat_send.at[target], stat_recv.at[me],
            {"tm": tt, "space": ss, "chan": core},
        )

    def stat_from(tt, ss, core):
        source = (tt * n_space + ss) * 2 + core
        return remote(
            stat, stats.at[source], stat_send.at[source], stat_recv.at[source],
            {"tm": tt, "space": ss, "chan": core},
        )

    def each_stat(act):
        @pl.loop(0, n_tm)
        def _(step):
            far = n_tm - 1 - step
            for up in (True, False):
                tt = t + far if up else t - far
                ok = jnp.logical_and(tt < n_tm, tt >= 0)
                if not up:
                    ok = jnp.logical_and(ok, far > 0)
                for ss in range(n_space):
                    for core in range(2):
                        use = jnp.logical_and(ok, needs(tt, ss, core))
                        other = (tt * n_space + ss) * 2 + core != me

                        @pl.when(jnp.logical_and(use, other))
                        def _(tt=tt, ss=ss, core=core):
                            act(tt, ss, core)

    each_stat(lambda tt, ss, core: stat_copy(tt, ss, core).start())

    spread_row = lax.broadcasted_iota(jnp.int32, (columns, lanes), 0)
    spread_col = lax.broadcasted_iota(jnp.int32, (columns, lanes), 1)
    spread = jnp.where(spread_row == 2 * spread_col, 1.0, 0.0).astype(BF16)
    weights = jnp.concatenate(
        [
            jnp.concatenate([out_weight[2 * i + j] for i in range(2)], axis=1)
            for j in range(2)
        ],
        axis=0,
    )

    each_stat(lambda tt, ss, core: stat_from(tt, ss, core).wait_recv())

    owners = [
        pltpu.make_async_copy(stats.at[(b * n_space + s) * 2 + c], ids.at[b], local_sem.at[8])
        for b in range(n_tm)
    ]
    for copy in owners:
        copy.start()

    sizes_row = jnp.where(
        row8 == 2, float(rows * columns), float(half_rows * columns)
    )
    is_size = jnp.logical_or(row8 == 2, row8 == 5)

    def add_source(source, carry, clip):
        value = stats[source]
        key = jnp.where(row8 < 3, value[2:3], value[5:6])
        value = jnp.where(is_size, sizes_row, value)
        return carry + jnp.where(key == clip, value, 0.0)

    def moments_of(clip):
        clip = clip.astype(F32)
        found = jnp.zeros((8, 128), F32)
        if total <= 32:
            for source in range(total):
                found = add_source(source, found, clip)
        else:
            found = lax.fori_loop(
                0, total, lambda source, carry: add_source(source, carry, clip), found
            )
        found = found + pltpu.roll(found, 5, 0)
        found = found + jnp.where(
            lane8 % 2 == 0, pltpu.roll(found, 127, 1), pltpu.roll(found, 1, 1)
        )
        found = found + jnp.where(
            lane8 % 4 < 2, pltpu.roll(found, 126, 1), pltpu.roll(found, 2, 1)
        )
        count = found[2:3]
        mean = found[0:1] / count
        var = found[1:2] / count - mean * mean
        scale = lax.rsqrt(var + 1e-6) * gain[...] * 0.5
        shift = bias[...] * 0.5 - mean * scale
        return jnp.broadcast_to(scale, (128, 128)).T, jnp.broadcast_to(shift, (128, 128)).T

    def finish(kept, begin, scale_c, shift_c):
        packed = []
        for r in range(piece_rows):
            pair = []
            for i in range(2):
                value = conv[kept, 2 * (begin + r) + i].astype(F32)
                pieces = []
                for u in range(2):
                    v = value[:, u * lanes:(u + 1) * lanes] * scale_c + shift_c
                    pieces.append((v + v * jnp.tanh(v)).astype(BF16))
                pair.append(jnp.concatenate(pieces, axis=1))
            both = jnp.dot(
                weights, jnp.concatenate(pair, axis=0), preferred_element_type=F32
            )
            packed.append((both[0:32] + pltpu.roll(both[32:64], columns - 1, 1)).astype(BF16))
        result = jnp.dot(
            jnp.concatenate(packed, axis=0), spread, preferred_element_type=F32
        ).astype(BF16)
        for r in range(piece_rows):
            for core in range(2):
                latent[kept, core, begin + r] = result[r * 32 + core * 16:r * 32 + core * 16 + 16]

    def send_latent(kept, begin, frame):
        span = pl.ds(frame * lat_rows + begin, piece_rows)
        arrived[span] = latent[kept, c, pl.ds(begin, piece_rows)]

        @pl.loop(0, n_tm)
        def _(step):
            far = n_tm - 1 - step
            for up in (True, False):
                tt = t + far if up else t - far
                ok = jnp.logical_and(tt < n_tm, tt >= 0)
                if not up:
                    ok = jnp.logical_and(ok, far > 0)
                for core in range(2):
                    other = jnp.logical_or(tt != t, core != c)

                    @pl.when(jnp.logical_and(ok, other))
                    def _(tt=tt, core=core):
                        remote(
                            latent.at[kept, core, pl.ds(begin, piece_rows)], arrived.at[span],
                            lat_send.at[kept], lat_recv.at[0],
                            {"tm": tt, "space": s, "chan": core},
                        ).start()

    my_frame = 2 * t + 2 - c

    @pl.when(first)
    def _():
        finish(1, half_index * piece_rows, *moments_of(clip_in[0, 0]))
        send_latent(1, half_index * piece_rows, 0)

    @pl.when(has_main)
    def _():
        found = moments_of(my_clip)
        for piece in range(2):
            finish(0, piece * piece_rows, *found)
            send_latent(0, piece * piece_rows, my_frame)

    pltpu.make_async_copy(stats.at[pl.ds(0, n_tm)], ids, local_sem.at[8]).wait()

    def arrived_wait(count):
        span = arrived.at[pl.ds(0, count)]
        remote(
            span, span, lat_send.at[0], lat_recv.at[0], {"tm": t, "space": s, "chan": c}
        ).wait_recv()

    every = n_frames * lat_rows

    @pl.when(first)
    def _():
        arrived_wait(every - lat_rows - piece_rows)

    @pl.when(jnp.logical_and(has_main, t > 0))
    def _():
        arrived_wait(every - lat_rows)

    @pl.when(jnp.logical_not(has_main))
    def _():
        arrived_wait(every)

    here = t.astype(F32)

    @pl.loop(0, n_tm)
    def _(b):
        taken = jnp.int32(0)
        slots = []
        for n in range(own_rows):
            hit = ids[b, 6, n] == here
            slots.append(jnp.where(hit, taken, -1))
            taken = taken + jnp.where(hit, 1, 0)
        for j in range(capacity):
            value = jnp.zeros((16, lanes), BF16)
            for n in range(own_rows):
                value = jnp.where(slots[n] == j, arrived[b * own_rows + n], value)
            out[0, b * capacity + j] = value

    peer.wait_send()
    for up, ok in zs:
        @pl.when(ok)
        def _(up=up):
            for p in range(rows - window, rows):
                z_copy(up, p, 1).wait_send()
            meta_copy(up).wait_send()
    for low, ok in sides:
        @pl.when(ok)
        def _(low=low):
            there = x.at[pl.ds(0, 2), 0]
            remote(
                there, there, edge_send.at[int(low)], edge_recv.at[int(low)],
                {"tm": t, "space": s, "chan": c},
            ).wait_send()

            @pl.when(gets_z)
            def _():
                forward(low).wait_send()

    each_stat(lambda tt, ss, core: stat_copy(tt, ss, core).wait_send())

    def latents_left(kept, count):
        span = arrived.at[pl.ds(0, count)]
        remote(
            span, span, lat_send.at[kept], lat_recv.at[0], {"tm": t, "space": s, "chan": c}
        ).wait_send()

    @pl.when(first)
    def _():
        latents_left(1, (2 * n_tm - 1) * piece_rows)

    @pl.when(has_main)
    def _():
        latents_left(0, (2 * n_tm - 1) * lat_rows)


def solution(mesh):
    n_tm, n_space = mesh.shape["tm"], mesh.shape["space"]
    total = n_tm * n_space * 2

    def shards(activations, frame_clip, conv_weight, norm_gain, norm_bias, out_weight, owner):
        half, frames_here, rows, columns = activations.shape
        lat_rows = rows // 2
        capacity = max(2, 2 * frames_here * lat_rows // n_tm)
        moments = out_weight.shape[-1]
        dma = pltpu.SemaphoreType.DMA
        return pl.pallas_call(
            functools.partial(kernel, (n_tm, n_space, capacity)),
            out_shape=jax.ShapeDtypeStruct(
                (1, n_tm * capacity, moments // 2, columns // 2), BF16
            ),
            in_specs=[pl.BlockSpec(memory_space=pltpu.HBM)] * 7,
            out_specs=pl.BlockSpec(memory_space=pltpu.VMEM),
            scratch_shapes=[
                pltpu.SMEM((1, frames_here), jnp.int32),
                pltpu.SMEM((1, frames_here * lat_rows), jnp.int32),
                pltpu.VMEM(activations.shape, BF16),
                pltpu.VMEM(conv_weight.shape, BF16),
                pltpu.VMEM((1, CHANNELS), F32),
                pltpu.VMEM((1, CHANNELS), F32),
                pltpu.VMEM((4, moments, CHANNELS), BF16),
                pltpu.VMEM((8, 128), jnp.int32),
                pltpu.VMEM((2, 8, 128), jnp.int32),
                pltpu.SMEM((2, 8, 128), jnp.int32),
                pltpu.VMEM((3, rows + 2, 2, half, columns), BF16),
                pltpu.VMEM((384, 1152), BF16),
                pltpu.VMEM((2, rows, CHANNELS, columns), BF16),
                pltpu.VMEM((8, 128), F32),
                pltpu.VMEM((total, 8, 128), F32),
                pltpu.SMEM((n_tm, 8, 128), F32),
                pltpu.VMEM((2, 2, lat_rows, moments // 2, columns // 2), BF16),
                pltpu.VMEM((n_tm * frames_here * lat_rows, moments // 2, columns // 2), BF16),
                pltpu.VMEM((2, CHANNELS, columns // 2), F32),
                pltpu.SemaphoreType.REGULAR((2,)),
                dma((2, 4)),
                dma((rows,)),
                dma((2,)),
                dma((2,)),
                dma((2,)),
                dma((2,)),
                dma((1,)),
                dma((1,)),
                dma((2,)),
                dma((2,)),
                dma((total,)),
                dma((total,)),
                dma((2,)),
                dma((1,)),
                dma((9,)),
            ],
            compiler_params=pltpu.CompilerParams(
                collective_id=0, has_side_effects=True, vmem_limit_bytes=24 * 1024 * 1024
            ),
        )(*(
            pltpu.with_memory_space_constraint(operand, pltpu.HBM)
            for operand in (
                frame_clip.reshape(1, -1), owner.reshape(1, -1), activations, conv_weight,
                norm_gain.reshape(1, -1), norm_bias.reshape(1, -1),
                out_weight.transpose(0, 1, 3, 2).reshape(4, moments, CHANNELS),
            )
        ))

    placed = (
        P(("groups", "chan"), "tm", "space", None),
        P(("groups", "tm")),
        P(),
        P(),
        P(),
        P(),
        P(("groups", "space"), "tm", None),
    )
    return jax.shard_map(
        shards,
        mesh=mesh,
        in_specs=placed,
        out_specs=P(("groups", "space"), "tm", "chan", None),
        check_vma=False,
    )
```

```python
import functools

import jax
import jax.numpy as jnp
from jax import lax
from jax.experimental import pallas as pl
from jax.experimental.pallas import tpu as pltpu
from jax.sharding import PartitionSpec as P

CHANNELS = 128
GROUPS = 32
GROUP_SIZE = CHANNELS // GROUPS
F32 = jnp.float32
BF16 = jnp.bfloat16
MESH = pl.DeviceIdType.MESH


def kernel(
    sizes, clip_hbm, owner_hbm, act_in, weight_in, gain_in, bias_in, out_weight_in, out,
    clip_in, owner_in, act_raw, weight, gain, bias, out_weight, meta_in, near_meta, near_ids, meta,
    x, wt, conv, stat, stats, ids, latent, arrived, sums,
    round_sem, z_send, z_recv, edge_send, edge_recv, fwd_send, fwd_recv, peer_send, peer_recv,
    meta_send, meta_recv, owner_send, owner_recv, stat_send, stat_recv, lat_send, lat_recv, local_sem,
):
    n_tm, n_space, capacity = sizes
    half, frames_here, rows, columns = act_raw.shape
    lanes = columns // 2
    total = n_tm * n_space * 2
    n_frames = n_tm * frames_here
    lat_rows = rows // 2
    own_rows = frames_here * lat_rows
    piece_rows = lat_rows // 2
    half_rows = rows // 2
    t = lax.axis_index("tm")
    s = lax.axis_index("space")
    c = lax.axis_index("chan")
    me = (t * n_space + s) * 2 + c
    first = t == 0
    has_main = jnp.logical_or(c == 1, t < n_tm - 1)
    mirror = n_space == 2
    flip = s == 0 if mirror else False
    rounds = max(n_tm // 2 + n_space - 1, n_tm - 1) - 1

    def repeat(count, body):
        if count <= 4:
            for n in range(count):
                body(n)
        else:
            pl.loop(0, count)(body)

    def row_of(p):
        return jnp.where(flip, rows - 1 - p, p) if mirror else p

    fetches = [
        pltpu.make_async_copy(source, held, local_sem.at[n])
        for n, (source, held) in enumerate((
            (act_in, act_raw), (clip_hbm, clip_in), (owner_hbm, owner_in), (weight_in, weight),
            (gain_in, gain), (bias_in, bias), (out_weight_in, out_weight),
        ))
    ]
    for fetch in fetches[:3]:
        fetch.start()
    stats[...] = jnp.full(stats.shape, -1.0, F32)

    up_ok, down_ok = t < n_tm - 1, t > 0
    low_ok, high_ok = s > 0, s < n_space - 1
    t_up, t_down = jnp.minimum(t + 1, n_tm - 1), jnp.maximum(t - 1, 0)
    s_low, s_high = jnp.maximum(s - 1, 0), jnp.minimum(s + 1, n_space - 1)
    around = [(up_ok, t_up, s), (down_ok, t_down, s), (low_ok, t, s_low), (high_ok, t, s_high)]
    near_count = jnp.int32(1)
    for ok, _, _ in around:
        near_count = near_count + jnp.where(ok, 2, 0)

    def greet(semaphore):
        for ok, tt, ss in around:
            @pl.when(ok)
            def _(tt=tt, ss=ss):
                for core in range(2):
                    pl.semaphore_signal(
                        semaphore, inc=1, device_id={"tm": tt, "space": ss, "chan": core},
                        device_id_type=MESH,
                    )
        pl.semaphore_signal(
            semaphore, inc=1, device_id={"tm": t, "space": s, "chan": 1 - c}, device_id_type=MESH
        )

    barrier = pltpu.get_barrier_semaphore()
    greet(barrier)

    zero_row = jnp.zeros((3, 2, half, columns), BF16)

    @pl.when(s == 0)
    def _():
        x[:, 0] = zero_row

    @pl.when(s == n_space - 1)
    def _():
        x[:, rows + 1] = zero_row

    fetches[1].wait()
    fetches[2].wait()
    place = lax.broadcasted_iota(jnp.int32, (8, 128), 1)
    numbers = jnp.zeros((8, 128), jnp.int32)
    for n in range(frames_here):
        numbers = jnp.where(place == n, clip_in[0, n], numbers)
    for n in range(own_rows):
        numbers = jnp.where(place == frames_here + n, owner_in[0, n], numbers)
    meta_in[...] = numbers
    meta[t] = numbers

    @pl.when(first)
    def _():
        near_meta[0] = numbers

    @pl.when(t == n_tm - 1)
    def _():
        near_meta[1] = numbers

    split_row = lax.broadcasted_iota(jnp.int32, (columns, columns), 0)
    split_col = lax.broadcasted_iota(jnp.int32, (columns, columns), 1)
    picked = jnp.where(split_col < lanes, 2 * split_col, 2 * (split_col - lanes) + 1)
    split = jnp.where(split_row == picked, 1.0, 0.0).astype(BF16)

    fetches[0].wait()
    for fetch in fetches[3:]:
        fetch.start()
    for f in range(frames_here):
        turned = jnp.transpose(act_raw[:, f], (1, 0, 2)).reshape(rows * half, columns)
        x[c + f, pl.ds(1, rows), c] = jnp.dot(
            turned, split, preferred_element_type=F32
        ).astype(BF16).reshape(rows, half, columns)

    pl.semaphore_wait(barrier, near_count)

    def remote(src, dst, send, recv, device):
        return pltpu.make_async_remote_copy(
            src_ref=src, dst_ref=dst, send_sem=send, recv_sem=recv, device_id=device,
            device_id_type=MESH,
        )

    def z_copy(up, p, count):
        frame, slot, core, tt = (1, 0, 1, t_up) if up else (0, 2, 0, t_down)
        begin = 1 + (jnp.where(flip, rows - p - count, p) if mirror else p)
        return remote(
            x.at[c + frame, pl.ds(begin, count), c], x.at[slot, pl.ds(begin, count), c],
            z_send.at[int(up)], z_recv.at[p], {"tm": tt, "space": s, "chan": core},
        )

    def meta_copy(up):
        return remote(
            meta_in, near_meta.at[0 if up else 1], meta_send.at[int(up)],
            meta_recv.at[0 if up else 1],
            {"tm": t_up if up else t_down, "space": s, "chan": c},
        )

    def edge(low, core):
        return remote(
            x.at[pl.ds(c, 2), 1 if low else rows, c],
            x.at[pl.ds(core, 2), rows + 1 if low else 0, c],
            edge_send.at[int(low)], edge_recv.at[int(low)],
            {"tm": t, "space": s_low if low else s_high, "chan": core},
        )

    z_slot = 2 * (1 - c)

    def forward(low):
        return remote(
            x.at[z_slot, 1 if low else rows], x.at[z_slot, rows + 1 if low else 0],
            fwd_send.at[int(low)], fwd_recv.at[int(low)],
            {"tm": t, "space": s_low if low else s_high, "chan": c},
        )

    peer = remote(
        x.at[pl.ds(c, 2), pl.ds(1, rows), c], x.at[pl.ds(1 - c, 2), pl.ds(1, rows), c],
        peer_send.at[0], peer_recv.at[0], {"tm": t, "space": s, "chan": 1 - c},
    )
    zs = ((True, up_ok), (False, down_ok))
    sides = ((True, low_ok), (False, high_ok))

    def start_z(p):
        for up, ok in zs:
            @pl.when(ok)
            def _(up=up):
                z_copy(up, p, 1).start()

    for up, ok in zs:
        @pl.when(ok)
        def _(up=up):
            meta_copy(up).start()
    peer.start()
    start_z(0)
    start_z(1)
    for low, ok in sides:
        @pl.when(ok)
        def _(low=low):
            edge(low, 0).start()
            edge(low, 1).start()
    for p in range(2, rows):
        start_z(p)

    if rounds > 0:
        greet(round_sem.at[0])

    fetches[3].wait()
    for k in range(3):
        for i in range(3):
            for j in range(3):
                wt[pl.ds(j * 128, 128), pl.ds((3 * k + i) * 128, 128)] = weight[k, i, j].T
    for fetch in fetches[4:]:
        fetch.wait()

    for up, ok in zs:
        @pl.when(ok)
        def _(up=up):
            meta_copy(not up).wait_recv()
    to_scalars = pltpu.make_async_copy(near_meta, near_ids, local_sem.at[7])
    to_scalars.start()
    to_scalars.wait()

    my_clip = jnp.where(c == 1, clip_in[0, 1], near_ids[1, 0, 0])
    newer = jnp.where(c == 1, clip_in[0, 0], clip_in[0, 1]) == my_clip
    older = jnp.logical_and(
        jnp.logical_or(c == 0, t > 0),
        jnp.where(c == 1, near_ids[0, 0, 1], clip_in[0, 0]) == my_clip,
    )

    peer.wait_recv()
    if rounds > 0:
        pl.semaphore_wait(round_sem.at[0], near_count)

        @pl.loop(1, rounds)
        def _(r):
            greet(round_sem.at[lax.rem(r, 2)])

            @pl.when(r < rounds - 1)
            def _():
                pl.semaphore_wait(round_sem.at[lax.rem(r, 2)], near_count)

    lane = lax.broadcasted_iota(jnp.int32, (CHANNELS, lanes), 1)

    def conv_row(h, kept, taps):
        acc = jnp.dot(
            wt[...], jnp.concatenate([tap(h) for tap in taps], axis=0),
            preferred_element_type=F32,
        )
        even, odd = acc[:, :lanes], acc[:, lanes:]
        before = jnp.where(lane == 0, 0.0, pltpu.roll(odd[0:128], 1, 1))
        after = jnp.where(lane == lanes - 1, 0.0, pltpu.roll(even[256:384], lanes - 1, 1))
        even, odd = (
            (before + even[128:256] + odd[256:384]).astype(BF16),
            (even[0:128] + odd[128:256] + after).astype(BF16),
        )
        conv[kept, h] = jnp.concatenate([even, odd], axis=1)
        a, b = even.astype(F32), odd.astype(F32)
        return a + b, a * a + b * b

    def conv_rows(places, kept, taps):
        found = [conv_row(h, kept, taps) for h in places]
        for q in range(2):
            total_q = found[0][q]
            for one in found[1:]:
                total_q = total_q + one[q]
            sums[q] += total_q

    def slab(slot):
        return lambda h: x[slot, pl.ds(h, 3)].reshape(3 * CHANNELS, columns)

    def sums_to(row):
        stat[pl.ds(row, 1), :] = jnp.sum(sums[0].T, axis=0, keepdims=True)
        stat[pl.ds(row + 1, 1), :] = jnp.sum(sums[1].T, axis=0, keepdims=True)

    def wait_edges():
        for low, ok in ((True, high_ok), (False, low_ok)):
            @pl.when(ok)
            def _(low=low):
                there = x.at[pl.ds(c, 2), rows + 1 if low else 0]
                remote(
                    there, there, edge_send.at[int(low)], edge_recv.at[int(low)],
                    {"tm": t, "space": s, "chan": c},
                ).wait_recv()

    gets_z = jnp.logical_or(jnp.logical_and(c == 1, down_ok), jnp.logical_and(c == 0, up_ok))

    def wait_z(p):
        @pl.when(gets_z)
        def _():
            there = x.at[z_slot, pl.ds(1 + row_of(p), 1)]
            remote(
                there, there, z_send.at[0], z_recv.at[p], {"tm": t, "space": s, "chan": c}
            ).wait_recv()

    def start_forwards():
        for low, ok in sides:
            @pl.when(jnp.logical_and(gets_z, ok))
            def _(low=low):
                forward(low).start()

    def wait_forwards():
        for low, ok in ((True, high_ok), (False, low_ok)):
            @pl.when(jnp.logical_and(gets_z, ok))
            def _(low=low):
                forward(low).wait_recv()

    row8 = lax.broadcasted_iota(jnp.int32, (8, 128), 0)
    lane8 = lax.broadcasted_iota(jnp.int32, (8, 128), 1)
    facts = jnp.where(row8 == 2, jnp.where(has_main, my_clip, -1).astype(F32), -1.0)
    facts = jnp.where(
        jnp.logical_and(row8 == 5, first), clip_in[0, 0].astype(F32), facts
    )
    stat[...] = facts

    half_index = jnp.where(flip, c, 1 - c) if mirror else c

    if not mirror:
        wait_edges()

    @pl.when(first)
    def _():
        sums[...] = jnp.zeros_like(sums)

        if mirror:
            @pl.when(c == 1)
            def _():
                wait_edges()
        begin = jnp.where(c == 0, half_rows, 0) if mirror else c * half_rows
        conv_rows(
            [row_of(begin + p) for p in range(half_rows - 1, -1, -1)], 1, [slab(c)] * 3
        )
        sums_to(3)

    def tap_old(h):
        return jnp.where(older, slab(0)(h), tap_mid(h))

    def tap_mid(h):
        return jnp.where(newer, slab(1)(h), slab(2)(h))

    taps = [tap_old, tap_mid, slab(2)]
    steps = rows // 2

    def send_owners():
        def to(n):
            remote(
                meta_in, meta.at[t], owner_send.at[0], owner_recv.at[0],
                {"tm": lax.rem(t + 1 + n, n_tm), "space": s, "chan": c},
            ).start()

        repeat(n_tm - 1, to)

    def owner_wait(received):
        span = meta.at[pl.ds(0, n_tm - 1)]
        copy = remote(
            span, span, owner_send.at[0], owner_recv.at[0], {"tm": t, "space": s, "chan": c}
        )
        copy.wait_recv() if received else copy.wait_send()

    if mirror:
        wait_z(0)
        start_forwards()
        wait_z(1)
    else:
        for p in range(rows):
            wait_z(p)
        start_forwards()
        wait_forwards()

    sums[...] = jnp.zeros_like(sums)

    @pl.loop(0, steps - 2)
    def _(n):
        if mirror:
            wait_z(2 * n + 2)
            wait_z(2 * n + 3)

        @pl.when(has_main)
        def _():
            conv_rows([row_of(2 * n + 1), row_of(2 * n + 2)], 0, taps)

    if mirror:
        @pl.when(jnp.logical_not(jnp.logical_and(first, c == 1)))
        def _():
            wait_edges()
        wait_z(rows - 2)
        wait_forwards()
        wait_z(rows - 1)

    @pl.when(has_main)
    def _():
        conv_rows([row_of(p) for p in (rows - 3, 0, rows - 2, rows - 1)], 0, taps)

    @pl.when(has_main)
    def _():
        sums_to(0)

    stats[me] = stat[...]
    if rounds > 1:
        pl.semaphore_wait(round_sem.at[(rounds - 1) % 2], near_count)

    def stat_copy(tt, ss, core):
        return remote(
            stat, stats.at[me], stat_send.at[0], stat_recv.at[0],
            {"tm": tt, "space": ss, "chan": core},
        )

    reach = n_tm // 2

    def spaces(act):
        repeat(n_space, lambda n: act(lax.rem(s + n_space - 1 - n, n_space), n))

    far_t = jnp.where(c == 0, t + reach, t - reach)

    @pl.when(jnp.logical_and(far_t >= 0, far_t < n_tm))
    def _():
        spaces(lambda ss, n: stat_copy(far_t, ss, 1 - c).start())

    def slab_both(away):
        for tt in (t + away, t - away):
            @pl.when(jnp.logical_and(tt >= 0, tt < n_tm))
            def _(tt=tt):
                for core in range(2):
                    spaces(lambda ss, n: stat_copy(tt, ss, core).start())

    repeat(reach - 1, lambda n: slab_both(reach - 1 - n))
    repeat(n_space - 1, lambda n: [
        stat_copy(t, lax.rem(s + 1 + n, n_space), core).start() for core in range(2)
    ] and None)
    stat_copy(t, s, 1 - c).start()
    send_owners()

    stat_counts = {
        (tt, core): 2 * n_space - 1 + sum(
            n_space * len([o for o in (0, 1) if abs(2 * (other - tt) + core - o) < n_tm])
            for other in range(n_tm) if other != tt
        )
        for tt in range(n_tm) for core in range(2)
    }

    def stat_wait(received):
        for count in sorted(set(stat_counts.values())):
            same = False
            for (tt, core), number in stat_counts.items():
                if number == count:
                    same = jnp.logical_or(same, jnp.logical_and(t == tt, c == core))

            @pl.when(same)
            def _(count=count):
                span = stats.at[pl.ds(0, count)]
                copy = remote(
                    span, span, stat_send.at[0], stat_recv.at[0],
                    {"tm": t, "space": s, "chan": c},
                )
                copy.wait_recv() if received else copy.wait_send()

    weights = jnp.concatenate([out_weight[q] for q in range(4)], axis=1)

    stat_wait(True)

    sizes_row = jnp.where(
        row8 == 2, float(rows * columns), float(half_rows * columns)
    )
    is_size = jnp.logical_or(row8 == 2, row8 == 5)

    def add_source(source, carry, clip):
        value = stats[source]
        key = jnp.where(row8 < 3, value[2:3], value[5:6])
        value = jnp.where(is_size, sizes_row, value)
        return carry + jnp.where(key == clip, value, 0.0)

    def moments_of(clip):
        clip = clip.astype(F32)
        found = jnp.zeros((8, 128), F32)
        if total <= 32:
            for source in range(total):
                found = add_source(source, found, clip)
        else:
            found = lax.fori_loop(
                0, total, lambda source, carry: add_source(source, carry, clip), found
            )
        found = found + pltpu.roll(found, 5, 0)
        found = found + jnp.where(
            lane8 % 2 == 0, pltpu.roll(found, 127, 1), pltpu.roll(found, 1, 1)
        )
        found = found + jnp.where(
            lane8 % 4 < 2, pltpu.roll(found, 126, 1), pltpu.roll(found, 2, 1)
        )
        count = found[2:3]
        mean = found[0:1] / count
        var = found[1:2] / count - mean * mean
        scale = lax.rsqrt(var + 1e-6) * gain[...] * 0.5
        shift = bias[...] * 0.5 - mean * scale
        return jnp.broadcast_to(scale, (128, 128)).T, jnp.broadcast_to(shift, (128, 128)).T

    def finish(kept, begin, count, scale_c, shift_c):
        wide = []
        for r in range(count):
            pieces = []
            for i in range(2):
                value = conv[kept, 2 * (begin + r) + i].astype(F32)
                for j in range(2):
                    v = value[:, j * lanes:(j + 1) * lanes] * scale_c + shift_c
                    pieces.append((v + v * jnp.tanh(v)).astype(BF16))
            wide.append(jnp.concatenate(pieces, axis=0))
        result = jnp.dot(
            weights, jnp.concatenate(wide, axis=1), preferred_element_type=F32
        ).astype(BF16)
        for r in range(count):
            for core in range(2):
                latent[kept, core, begin + r] = result[
                    core * 16:core * 16 + 16, r * lanes:(r + 1) * lanes
                ]

    def send_latent(kept, begin, count, frame):
        span = pl.ds(frame * lat_rows + begin, count)
        arrived[span] = latent[kept, c, pl.ds(begin, count)]

        def to(tt, core):
            remote(
                latent.at[kept, core, pl.ds(begin, count)], arrived.at[span],
                lat_send.at[kept], lat_recv.at[0], {"tm": tt, "space": s, "chan": core},
            ).start()

        def others(n):
            step = jnp.where(t < n_tm // 2, n_tm - 1 - n, 1 + n)
            for core in range(2):
                to(lax.rem(t + step, n_tm), core)

        repeat(n_tm - 1, others)
        to(t, 1 - c)

    my_frame = 2 * t + 2 - c

    @pl.when(first)
    def _():
        finish(1, half_index * piece_rows, piece_rows, *moments_of(clip_in[0, 0]))
        send_latent(1, half_index * piece_rows, piece_rows, 0)

    @pl.when(has_main)
    def _():
        found = moments_of(my_clip)
        finish(0, 0, lat_rows, *found)
        send_latent(0, 0, lat_rows, my_frame)

    owner_wait(True)
    owners = pltpu.make_async_copy(meta, ids, local_sem.at[8])
    owners.start()
    owners.wait()

    def arrived_wait(count):
        span = arrived.at[pl.ds(0, count)]
        remote(
            span, span, lat_send.at[0], lat_recv.at[0], {"tm": t, "space": s, "chan": c}
        ).wait_recv()

    every = n_frames * lat_rows

    @pl.when(first)
    def _():
        arrived_wait(every - lat_rows - piece_rows)

    @pl.when(jnp.logical_and(has_main, t > 0))
    def _():
        arrived_wait(every - lat_rows)

    @pl.when(jnp.logical_not(has_main))
    def _():
        arrived_wait(every)

    @pl.loop(0, n_tm)
    def _(b):
        taken = jnp.int32(0)
        slots = []
        for n in range(own_rows):
            hit = ids[b, 0, frames_here + n] == t
            slots.append(jnp.where(hit, taken, -1))
            taken = taken + jnp.where(hit, 1, 0)
        for j in range(capacity):
            value = jnp.zeros((16, lanes), BF16)
            for n in range(own_rows):
                value = jnp.where(slots[n] == j, arrived[b * own_rows + n], value)
            out[0, b * capacity + j] = value

    peer.wait_send()
    for up, ok in zs:
        @pl.when(ok)
        def _(up=up):
            z_copy(up, 0, rows).wait_send()
            meta_copy(up).wait_send()
    for low, ok in sides:
        @pl.when(ok)
        def _(low=low):
            there = x.at[pl.ds(0, 2), 0]
            remote(
                there, there, edge_send.at[int(low)], edge_recv.at[int(low)],
                {"tm": t, "space": s, "chan": c},
            ).wait_send()

            @pl.when(gets_z)
            def _():
                forward(low).wait_send()

    stat_wait(False)
    owner_wait(False)

    def latents_left(kept, count):
        span = arrived.at[pl.ds(0, count)]
        remote(
            span, span, lat_send.at[kept], lat_recv.at[0], {"tm": t, "space": s, "chan": c}
        ).wait_send()

    @pl.when(first)
    def _():
        latents_left(1, (2 * n_tm - 1) * piece_rows)

    @pl.when(has_main)
    def _():
        latents_left(0, (2 * n_tm - 1) * lat_rows)


def solution(mesh):
    n_tm, n_space = mesh.shape["tm"], mesh.shape["space"]
    total = n_tm * n_space * 2

    def shards(activations, frame_clip, conv_weight, norm_gain, norm_bias, out_weight, owner):
        half, frames_here, rows, columns = activations.shape
        lat_rows = rows // 2
        capacity = max(2, 2 * frames_here * lat_rows // n_tm)
        moments = out_weight.shape[-1]
        dma = pltpu.SemaphoreType.DMA
        return pl.pallas_call(
            functools.partial(kernel, (n_tm, n_space, capacity)),
            out_shape=jax.ShapeDtypeStruct(
                (1, n_tm * capacity, moments // 2, columns // 2), BF16
            ),
            in_specs=[pl.BlockSpec(memory_space=pltpu.HBM)] * 7,
            out_specs=pl.BlockSpec(memory_space=pltpu.VMEM),
            scratch_shapes=[
                pltpu.SMEM((1, frames_here), jnp.int32),
                pltpu.SMEM((1, frames_here * lat_rows), jnp.int32),
                pltpu.VMEM(activations.shape, BF16),
                pltpu.VMEM(conv_weight.shape, BF16),
                pltpu.VMEM((1, CHANNELS), F32),
                pltpu.VMEM((1, CHANNELS), F32),
                pltpu.VMEM((4, moments, CHANNELS), BF16),
                pltpu.VMEM((8, 128), jnp.int32),
                pltpu.VMEM((2, 8, 128), jnp.int32),
                pltpu.SMEM((2, 8, 128), jnp.int32),
                pltpu.VMEM((n_tm, 8, 128), jnp.int32),
                pltpu.VMEM((3, rows + 2, 2, half, columns), BF16),
                pltpu.VMEM((384, 1152), BF16),
                pltpu.VMEM((2, rows, CHANNELS, columns), BF16),
                pltpu.VMEM((8, 128), F32),
                pltpu.VMEM((total, 8, 128), F32),
                pltpu.SMEM((n_tm, 8, 128), jnp.int32),
                pltpu.VMEM((2, 2, lat_rows, moments // 2, columns // 2), BF16),
                pltpu.VMEM((n_tm * frames_here * lat_rows, moments // 2, columns // 2), BF16),
                pltpu.VMEM((2, CHANNELS, columns // 2), F32),
                pltpu.SemaphoreType.REGULAR((2,)),
                dma((2,)),
                dma((rows,)),
                dma((2,)),
                dma((2,)),
                dma((2,)),
                dma((2,)),
                dma((1,)),
                dma((1,)),
                dma((2,)),
                dma((2,)),
                dma((1,)),
                dma((1,)),
                dma((1,)),
                dma((1,)),
                dma((2,)),
                dma((1,)),
                dma((9,)),
            ],
            compiler_params=pltpu.CompilerParams(
                collective_id=0, has_side_effects=True, vmem_limit_bytes=24 * 1024 * 1024
            ),
        )(*(
            pltpu.with_memory_space_constraint(operand, pltpu.HBM)
            for operand in (
                frame_clip.reshape(1, -1), owner.reshape(1, -1), activations, conv_weight,
                norm_gain.reshape(1, -1), norm_bias.reshape(1, -1),
                out_weight.transpose(0, 1, 3, 2).reshape(4, moments, CHANNELS),
            )
        ))

    placed = (
        P(("groups", "chan"), "tm", "space", None),
        P(("groups", "tm")),
        P(),
        P(),
        P(),
        P(),
        P(("groups", "space"), "tm", None),
    )
    return jax.shard_map(
        shards,
        mesh=mesh,
        in_specs=placed,
        out_specs=P(("groups", "space"), "tm", "chan", None),
        check_vma=False,
    )
```

```python
import functools

import jax
import jax.numpy as jnp
from jax import lax
from jax.experimental import pallas as pl
from jax.experimental.pallas import tpu as pltpu
from jax.sharding import PartitionSpec as P

CHANNELS = 128
GROUPS = 32
GROUP_SIZE = CHANNELS // GROUPS
F32 = jnp.float32
BF16 = jnp.bfloat16
MESH = pl.DeviceIdType.MESH


def kernel(
    sizes, clip_hbm, owner_hbm, act_in, weight_in, gain_in, bias_in, out_weight_in, out,
    clip_in, owner_in, act_raw, weight, gain, bias, out_weight, meta_in, near_meta, near_ids, meta,
    x, wt, wz, acc, conv, stat, stats, ids, latent, arrived, sums,
    round_sem, z_send, z_recv, edge_send, edge_recv, fwd_send, fwd_recv, peer_send, peer_recv,
    meta_send, meta_recv, owner_send, owner_recv, stat_send, stat_recv, lat_send, lat_recv, local_sem,
):
    n_tm, n_space, capacity = sizes
    half, frames_here, rows, columns = act_raw.shape
    lanes = columns // 2
    total = n_tm * n_space * 2
    n_frames = n_tm * frames_here
    lat_rows = rows // 2
    own_rows = frames_here * lat_rows
    piece_rows = lat_rows // 2
    half_rows = rows // 2
    t = lax.axis_index("tm")
    s = lax.axis_index("space")
    c = lax.axis_index("chan")
    me = (t * n_space + s) * 2 + c
    first = t == 0
    has_main = jnp.logical_or(c == 1, t < n_tm - 1)
    mirror = n_space == 2
    flip = s == 0 if mirror else False
    rounds = max(n_tm // 2 + n_space - 1, n_tm - 1) - 1

    def repeat(count, body):
        if count <= 4:
            for n in range(count):
                body(n)
        else:
            pl.loop(0, count)(body)

    def row_of(p):
        return jnp.where(flip, rows - 1 - p, p) if mirror else p

    fetches = [
        pltpu.make_async_copy(source, held, local_sem.at[n])
        for n, (source, held) in enumerate((
            (act_in, act_raw), (clip_hbm, clip_in), (owner_hbm, owner_in), (weight_in, weight),
            (gain_in, gain), (bias_in, bias), (out_weight_in, out_weight),
        ))
    ]
    for fetch in fetches[:3]:
        fetch.start()
    stats[...] = jnp.full(stats.shape, -1.0, F32)
    stat[...] = jnp.full(stat.shape, -1.0, F32)

    up_ok, down_ok = t < n_tm - 1, t > 0
    low_ok, high_ok = s > 0, s < n_space - 1
    t_up, t_down = jnp.minimum(t + 1, n_tm - 1), jnp.maximum(t - 1, 0)
    s_low, s_high = jnp.maximum(s - 1, 0), jnp.minimum(s + 1, n_space - 1)
    around = [(up_ok, t_up, s), (down_ok, t_down, s), (low_ok, t, s_low), (high_ok, t, s_high)]
    near_count = jnp.int32(1)
    for ok, _, _ in around:
        near_count = near_count + jnp.where(ok, 2, 0)

    def greet(semaphore):
        for ok, tt, ss in around:
            @pl.when(ok)
            def _(tt=tt, ss=ss):
                for core in range(2):
                    pl.semaphore_signal(
                        semaphore, inc=1, device_id={"tm": tt, "space": ss, "chan": core},
                        device_id_type=MESH,
                    )
        pl.semaphore_signal(
            semaphore, inc=1, device_id={"tm": t, "space": s, "chan": 1 - c}, device_id_type=MESH
        )

    barrier = pltpu.get_barrier_semaphore()
    greet(barrier)

    zero_row = jnp.zeros((3, 2, half, columns), BF16)

    @pl.when(s == 0)
    def _():
        x[:, 0] = zero_row

    @pl.when(s == n_space - 1)
    def _():
        x[:, rows + 1] = zero_row

    @pl.when(jnp.logical_and(first, c == 1))
    def _():
        x[0] = jnp.zeros((rows + 2, 2, half, columns), BF16)

    fetches[1].wait()
    fetches[2].wait()
    place = lax.broadcasted_iota(jnp.int32, (8, 128), 1)
    numbers = jnp.zeros((8, 128), jnp.int32)
    for n in range(frames_here):
        numbers = jnp.where(place == n, clip_in[0, n], numbers)
    for n in range(own_rows):
        numbers = jnp.where(place == frames_here + n, owner_in[0, n], numbers)
    meta_in[...] = numbers
    meta[t] = numbers

    gets_z = jnp.logical_or(
        jnp.logical_and(c == 0, up_ok), jnp.logical_and(c == 1, down_ok)
    )

    @pl.when(jnp.logical_not(gets_z))
    def _():
        near_meta[...] = numbers

    split_row = lax.broadcasted_iota(jnp.int32, (columns, columns), 0)
    split_col = lax.broadcasted_iota(jnp.int32, (columns, columns), 1)
    picked = jnp.where(split_col < lanes, 2 * split_col, 2 * (split_col - lanes) + 1)
    split = jnp.where(split_row == picked, 1.0, 0.0).astype(BF16)

    fetches[0].wait()
    for fetch in fetches[3:]:
        fetch.start()
    for f in range(frames_here):
        turned = jnp.transpose(act_raw[:, f], (1, 0, 2)).reshape(rows * half, columns)
        x[c + f, pl.ds(1, rows), c] = jnp.dot(
            turned, split, preferred_element_type=F32
        ).astype(BF16).reshape(rows, half, columns)

    pl.semaphore_wait(barrier, near_count)

    def remote(src, dst, send, recv, device):
        return pltpu.make_async_remote_copy(
            src_ref=src, dst_ref=dst, send_sem=send, recv_sem=recv, device_id=device,
            device_id_type=MESH,
        )

    def z_copy(up, p, count):
        frame, slot, core, tt = (1, 0, 1, t_up) if up else (0, 2, 0, t_down)
        begin = 1 + (jnp.where(flip, rows - p - count, p) if mirror else p)
        return remote(
            x.at[c + frame, pl.ds(begin, count), c], x.at[slot, pl.ds(begin, count), c],
            z_send.at[int(up)], z_recv.at[p], {"tm": tt, "space": s, "chan": core},
        )

    meta_copy = remote(
        meta_in, near_meta, meta_send.at[0], meta_recv.at[0],
        {"tm": jnp.where(c == 0, t_down, t_up), "space": s, "chan": c},
    )
    meta_sent = jnp.logical_or(
        jnp.logical_and(c == 0, down_ok), jnp.logical_and(c == 1, up_ok)
    )

    def edge(low, core):
        return remote(
            x.at[pl.ds(c, 2), 1 if low else rows, c],
            x.at[pl.ds(core, 2), rows + 1 if low else 0, c],
            edge_send.at[int(low)], edge_recv.at[int(low)],
            {"tm": t, "space": s_low if low else s_high, "chan": core},
        )

    z_slot = 2 * (1 - c)

    def forward(low):
        return remote(
            x.at[z_slot, 1 if low else rows], x.at[z_slot, rows + 1 if low else 0],
            fwd_send.at[int(low)], fwd_recv.at[int(low)],
            {"tm": t, "space": s_low if low else s_high, "chan": c},
        )

    peer = remote(
        x.at[pl.ds(c, 2), pl.ds(1, rows), c], x.at[pl.ds(1 - c, 2), pl.ds(1, rows), c],
        peer_send.at[0], peer_recv.at[0], {"tm": t, "space": s, "chan": 1 - c},
    )
    zs = ((True, up_ok), (False, down_ok))
    sides = ((True, low_ok), (False, high_ok))

    def start_z(p):
        for up, ok in zs:
            @pl.when(ok)
            def _(up=up):
                z_copy(up, p, 1).start()

    @pl.when(meta_sent)
    def _():
        meta_copy.start()

    peer.start()
    start_z(0)
    start_z(1)
    for low, ok in sides:
        @pl.when(ok)
        def _(low=low):
            edge(low, 0).start()
            edge(low, 1).start()
    for p in range(2, rows):
        start_z(p)

    if rounds > 0:
        greet(round_sem.at[0])

    fetches[3].wait()
    for k in range(3):
        for i in range(3):
            for j in range(3):
                wt[pl.ds(j * 128, 128), pl.ds((3 * k + i) * 128, 128)] = weight[k, i, j].T
    for fetch in fetches[4:]:
        fetch.wait()

    peer.wait_recv()
    if rounds > 0:
        pl.semaphore_wait(round_sem.at[0], near_count)

        @pl.loop(1, rounds)
        def _(r):
            greet(round_sem.at[lax.rem(r, 2)])

            @pl.when(r < rounds - 1)
            def _():
                pl.semaphore_wait(round_sem.at[lax.rem(r, 2)], near_count)

    lane = lax.broadcasted_iota(jnp.int32, (CHANNELS, lanes), 1)

    def own_taps(h):
        return jnp.dot(
            wt[...], jnp.concatenate([tap(h) for tap in taps_of_own], axis=0),
            preferred_element_type=F32,
        )

    def first_frame(h):
        seen = slab(c)(h)
        return jnp.dot(
            wt[...], jnp.concatenate([seen] * 3, axis=0), preferred_element_type=F32
        )

    def with_z(h):
        seen = slab(z_slot)(h)
        return acc[h] + jnp.dot(
            wz[...], jnp.concatenate([seen] * 2, axis=0), preferred_element_type=F32
        )

    def conv_row(h, kept, summed):
        found = summed(h)
        even, odd = found[:, :lanes], found[:, lanes:]
        before = jnp.where(lane == 0, 0.0, pltpu.roll(odd[0:128], 1, 1))
        after = jnp.where(lane == lanes - 1, 0.0, pltpu.roll(even[256:384], lanes - 1, 1))
        even, odd = (
            (before + even[128:256] + odd[256:384]).astype(BF16),
            (even[0:128] + odd[128:256] + after).astype(BF16),
        )
        conv[kept, h] = jnp.concatenate([even, odd], axis=1)
        a, b = even.astype(F32), odd.astype(F32)
        return a + b, a * a + b * b

    def conv_rows(places, kept, summed):
        found = [conv_row(h, kept, summed) for h in places]
        for q in range(2):
            total_q = found[0][q]
            for one in found[1:]:
                total_q = total_q + one[q]
            sums[q] += total_q

    def slab(slot):
        return lambda h: x[slot, pl.ds(h, 3)].reshape(3 * CHANNELS, columns)

    def sums_to(row):
        stat[pl.ds(row, 1), :] = jnp.sum(sums[0].T, axis=0, keepdims=True)
        stat[pl.ds(row + 1, 1), :] = jnp.sum(sums[1].T, axis=0, keepdims=True)

    def wait_edges():
        for low, ok in ((True, high_ok), (False, low_ok)):
            @pl.when(ok)
            def _(low=low):
                there = x.at[pl.ds(c, 2), rows + 1 if low else 0]
                remote(
                    there, there, edge_send.at[int(low)], edge_recv.at[int(low)],
                    {"tm": t, "space": s, "chan": c},
                ).wait_recv()

    def wait_z(p):
        @pl.when(gets_z)
        def _():
            there = x.at[z_slot, pl.ds(1 + row_of(p), 1)]
            remote(
                there, there, z_send.at[0], z_recv.at[p], {"tm": t, "space": s, "chan": c}
            ).wait_recv()

    def start_forwards():
        for low, ok in sides:
            @pl.when(jnp.logical_and(gets_z, ok))
            def _(low=low):
                forward(low).start()

    def wait_forwards():
        for low, ok in ((True, high_ok), (False, low_ok)):
            @pl.when(jnp.logical_and(gets_z, ok))
            def _(low=low):
                forward(low).wait_recv()

    half_index = jnp.where(flip, c, 1 - c) if mirror else c

    if not mirror:
        wait_edges()

    @pl.when(first)
    def _():
        sums[...] = jnp.zeros_like(sums)

        if mirror:
            @pl.when(c == 1)
            def _():
                wait_edges()
        begin = jnp.where(c == 0, half_rows, 0) if mirror else c * half_rows
        conv_rows(
            [row_of(begin + p) for p in range(half_rows - 1, -1, -1)], 1, first_frame
        )
        sums_to(3)

    @pl.when(gets_z)
    def _():
        meta_copy.wait_recv()

    to_scalars = pltpu.make_async_copy(near_meta, near_ids, local_sem.at[7])
    to_scalars.start()
    to_scalars.wait()

    my_clip = jnp.where(c == 1, clip_in[0, 1], near_ids[0, 0])
    newer = jnp.where(c == 1, clip_in[0, 0], clip_in[0, 1]) == my_clip
    older = jnp.logical_and(
        jnp.logical_or(c == 0, t > 0),
        jnp.where(c == 1, near_ids[0, 1], clip_in[0, 0]) == my_clip,
    )

    w_old, w_mid, w_new = (
        wt[:, pl.ds(k * 3 * CHANNELS, 3 * CHANNELS)].astype(F32) for k in range(3)
    )
    on_z = jnp.where(
        c == 0, w_new + jnp.where(newer, 0.0, w_mid + w_old), jnp.where(older, w_old, 0.0)
    )
    coarse = on_z.astype(BF16)
    wz[:, pl.ds(0, 3 * CHANNELS)] = coarse
    wz[:, pl.ds(3 * CHANNELS, 3 * CHANNELS)] = (on_z - coarse.astype(F32)).astype(BF16)

    row8 = lax.broadcasted_iota(jnp.int32, (8, 128), 0)
    lane8 = lax.broadcasted_iota(jnp.int32, (8, 128), 1)
    facts = jnp.where(row8 == 2, jnp.where(has_main, my_clip, -1).astype(F32), -1.0)
    facts = jnp.where(
        jnp.logical_and(row8 == 5, first), clip_in[0, 0].astype(F32), facts
    )
    stat[pl.ds(2, 1), :] = facts[2:3]
    stat[pl.ds(5, 1), :] = facts[5:6]

    none = jnp.zeros((3 * CHANNELS, columns), BF16)

    def newest(h):
        return jnp.where(c == 1, slab(1 + c)(h), none)

    def middle(h):
        return jnp.where(newer, slab(1)(h), newest(h))

    def oldest(h):
        return jnp.where(older, jnp.where(c == 0, slab(c)(h), none), middle(h))

    taps_of_own = [oldest, middle, newest]

    def own_rows_of(places):
        for p in places:
            h = row_of(p)
            acc[h] = own_taps(h)

    steps = rows // 2

    def send_owners():
        def to(n):
            remote(
                meta_in, meta.at[t], owner_send.at[0], owner_recv.at[0],
                {"tm": lax.rem(t + 1 + n, n_tm), "space": s, "chan": c},
            ).start()

        repeat(n_tm - 1, to)

    def owner_wait(received):
        span = meta.at[pl.ds(0, n_tm - 1)]
        copy = remote(
            span, span, owner_send.at[0], owner_recv.at[0], {"tm": t, "space": s, "chan": c}
        )
        copy.wait_recv() if received else copy.wait_send()

    tail = (rows - 3, 0, rows - 2, rows - 1)

    @pl.when(has_main)
    def _():
        own_rows_of(range(1, rows - 3))

    if mirror:
        wait_z(0)
        start_forwards()

        @pl.when(jnp.logical_not(jnp.logical_and(first, c == 1)))
        def _():
            wait_edges()
    else:
        for p in range(rows):
            wait_z(p)
        start_forwards()
        wait_forwards()

    @pl.when(has_main)
    def _():
        own_rows_of(tail)

    if mirror:
        wait_z(1)

    sums[...] = jnp.zeros_like(sums)

    @pl.loop(0, steps - 2)
    def _(n):
        if mirror:
            wait_z(2 * n + 2)
            wait_z(2 * n + 3)

        @pl.when(has_main)
        def _():
            conv_rows([row_of(2 * n + 1), row_of(2 * n + 2)], 0, with_z)

    if mirror:
        wait_z(rows - 2)
        wait_forwards()
        wait_z(rows - 1)

    @pl.when(has_main)
    def _():
        conv_rows([row_of(p) for p in tail], 0, with_z)

    @pl.when(has_main)
    def _():
        sums_to(0)

    stats[me] = stat[...]
    if rounds > 1:
        pl.semaphore_wait(round_sem.at[(rounds - 1) % 2], near_count)

    def stat_copy(tt, ss, core):
        return remote(
            stat, stats.at[me], stat_send.at[0], stat_recv.at[0],
            {"tm": tt, "space": ss, "chan": core},
        )

    reach = n_tm // 2

    def spaces(act):
        repeat(n_space, lambda n: act(lax.rem(s + n_space - 1 - n, n_space), n))

    far_t = jnp.where(c == 0, t + reach, t - reach)

    @pl.when(jnp.logical_and(far_t >= 0, far_t < n_tm))
    def _():
        spaces(lambda ss, n: stat_copy(far_t, ss, 1 - c).start())

    def slab_both(away):
        for tt in (t + away, t - away):
            @pl.when(jnp.logical_and(tt >= 0, tt < n_tm))
            def _(tt=tt):
                for core in range(2):
                    spaces(lambda ss, n: stat_copy(tt, ss, core).start())

    repeat(reach - 1, lambda n: slab_both(reach - 1 - n))
    repeat(n_space - 1, lambda n: [
        stat_copy(t, lax.rem(s + 1 + n, n_space), core).start() for core in range(2)
    ] and None)
    stat_copy(t, s, 1 - c).start()
    send_owners()

    stat_counts = {
        (tt, core): 2 * n_space - 1 + sum(
            n_space * len([o for o in (0, 1) if abs(2 * (other - tt) + core - o) < n_tm])
            for other in range(n_tm) if other != tt
        )
        for tt in range(n_tm) for core in range(2)
    }

    def stat_wait(received):
        for count in sorted(set(stat_counts.values())):
            same = False
            for (tt, core), number in stat_counts.items():
                if number == count:
                    same = jnp.logical_or(same, jnp.logical_and(t == tt, c == core))

            @pl.when(same)
            def _(count=count):
                span = stats.at[pl.ds(0, count)]
                copy = remote(
                    span, span, stat_send.at[0], stat_recv.at[0],
                    {"tm": t, "space": s, "chan": c},
                )
                copy.wait_recv() if received else copy.wait_send()

    weights = jnp.concatenate([out_weight[q] for q in range(4)], axis=1)

    stat_wait(True)

    sizes_row = jnp.where(
        row8 == 2, float(rows * columns), float(half_rows * columns)
    )
    is_size = jnp.logical_or(row8 == 2, row8 == 5)

    def add_source(source, carry, clip):
        value = stats[source]
        key = jnp.where(row8 < 3, value[2:3], value[5:6])
        value = jnp.where(is_size, sizes_row, value)
        return carry + jnp.where(key == clip, value, 0.0)

    def moments_of(clip):
        clip = clip.astype(F32)
        found = jnp.zeros((8, 128), F32)
        if total <= 32:
            for source in range(total):
                found = add_source(source, found, clip)
        else:
            found = lax.fori_loop(
                0, total, lambda source, carry: add_source(source, carry, clip), found
            )
        found = found + pltpu.roll(found, 5, 0)
        found = found + jnp.where(
            lane8 % 2 == 0, pltpu.roll(found, 127, 1), pltpu.roll(found, 1, 1)
        )
        found = found + jnp.where(
            lane8 % 4 < 2, pltpu.roll(found, 126, 1), pltpu.roll(found, 2, 1)
        )
        count = found[2:3]
        mean = found[0:1] / count
        var = found[1:2] / count - mean * mean
        scale = lax.rsqrt(var + 1e-6) * gain[...] * 0.5
        shift = bias[...] * 0.5 - mean * scale
        return jnp.broadcast_to(scale, (128, 128)).T, jnp.broadcast_to(shift, (128, 128)).T

    def finish(kept, begin, count, scale_c, shift_c):
        wide = []
        for r in range(count):
            pieces = []
            for i in range(2):
                value = conv[kept, 2 * (begin + r) + i].astype(F32)
                for j in range(2):
                    v = value[:, j * lanes:(j + 1) * lanes] * scale_c + shift_c
                    pieces.append((v + v * jnp.tanh(v)).astype(BF16))
            wide.append(jnp.concatenate(pieces, axis=0))
        result = jnp.dot(
            weights, jnp.concatenate(wide, axis=1), preferred_element_type=F32
        ).astype(BF16)
        for r in range(count):
            for core in range(2):
                latent[kept, core, begin + r] = result[
                    core * 16:core * 16 + 16, r * lanes:(r + 1) * lanes
                ]

    def send_latent(kept, begin, count, frame):
        span = pl.ds(frame * lat_rows + begin, count)
        arrived[span] = latent[kept, c, pl.ds(begin, count)]

        def to(tt, core):
            remote(
                latent.at[kept, core, pl.ds(begin, count)], arrived.at[span],
                lat_send.at[kept], lat_recv.at[0], {"tm": tt, "space": s, "chan": core},
            ).start()

        def others(n):
            step = jnp.where(t < n_tm // 2, n_tm - 1 - n, 1 + n)
            for core in range(2):
                to(lax.rem(t + step, n_tm), core)

        repeat(n_tm - 1, others)
        to(t, 1 - c)

    my_frame = 2 * t + 2 - c

    @pl.when(first)
    def _():
        finish(1, half_index * piece_rows, piece_rows, *moments_of(clip_in[0, 0]))
        send_latent(1, half_index * piece_rows, piece_rows, 0)

    @pl.when(has_main)
    def _():
        found = moments_of(my_clip)
        finish(0, 0, lat_rows, *found)
        send_latent(0, 0, lat_rows, my_frame)

    owner_wait(True)
    owners = pltpu.make_async_copy(meta, ids, local_sem.at[8])
    owners.start()
    owners.wait()

    def arrived_wait(count):
        span = arrived.at[pl.ds(0, count)]
        remote(
            span, span, lat_send.at[0], lat_recv.at[0], {"tm": t, "space": s, "chan": c}
        ).wait_recv()

    every = n_frames * lat_rows

    @pl.when(first)
    def _():
        arrived_wait(every - lat_rows - piece_rows)

    @pl.when(jnp.logical_and(has_main, t > 0))
    def _():
        arrived_wait(every - lat_rows)

    @pl.when(jnp.logical_not(has_main))
    def _():
        arrived_wait(every)

    @pl.loop(0, n_tm)
    def _(b):
        taken = jnp.int32(0)
        slots = []
        for n in range(own_rows):
            hit = ids[b, 0, frames_here + n] == t
            slots.append(jnp.where(hit, taken, -1))
            taken = taken + jnp.where(hit, 1, 0)
        for j in range(capacity):
            value = jnp.zeros((16, lanes), BF16)
            for n in range(own_rows):
                value = jnp.where(slots[n] == j, arrived[b * own_rows + n], value)
            out[0, b * capacity + j] = value

    peer.wait_send()
    for up, ok in zs:
        @pl.when(ok)
        def _(up=up):
            z_copy(up, 0, rows).wait_send()
    for low, ok in sides:
        @pl.when(ok)
        def _(low=low):
            there = x.at[pl.ds(0, 2), 0]
            remote(
                there, there, edge_send.at[int(low)], edge_recv.at[int(low)],
                {"tm": t, "space": s, "chan": c},
            ).wait_send()

            @pl.when(gets_z)
            def _():
                forward(low).wait_send()

    @pl.when(meta_sent)
    def _():
        meta_copy.wait_send()

    stat_wait(False)
    owner_wait(False)

    def latents_left(kept, count):
        span = arrived.at[pl.ds(0, count)]
        remote(
            span, span, lat_send.at[kept], lat_recv.at[0], {"tm": t, "space": s, "chan": c}
        ).wait_send()

    @pl.when(first)
    def _():
        latents_left(1, (2 * n_tm - 1) * piece_rows)

    @pl.when(has_main)
    def _():
        latents_left(0, (2 * n_tm - 1) * lat_rows)


def solution(mesh):
    n_tm, n_space = mesh.shape["tm"], mesh.shape["space"]
    total = n_tm * n_space * 2

    def shards(activations, frame_clip, conv_weight, norm_gain, norm_bias, out_weight, owner):
        half, frames_here, rows, columns = activations.shape
        lat_rows = rows // 2
        capacity = max(2, 2 * frames_here * lat_rows // n_tm)
        moments = out_weight.shape[-1]
        dma = pltpu.SemaphoreType.DMA
        return pl.pallas_call(
            functools.partial(kernel, (n_tm, n_space, capacity)),
            out_shape=jax.ShapeDtypeStruct(
                (1, n_tm * capacity, moments // 2, columns // 2), BF16
            ),
            in_specs=[pl.BlockSpec(memory_space=pltpu.HBM)] * 7,
            out_specs=pl.BlockSpec(memory_space=pltpu.VMEM),
            scratch_shapes=[
                pltpu.SMEM((1, frames_here), jnp.int32),
                pltpu.SMEM((1, frames_here * lat_rows), jnp.int32),
                pltpu.VMEM(activations.shape, BF16),
                pltpu.VMEM(conv_weight.shape, BF16),
                pltpu.VMEM((1, CHANNELS), F32),
                pltpu.VMEM((1, CHANNELS), F32),
                pltpu.VMEM((4, moments, CHANNELS), BF16),
                pltpu.VMEM((8, 128), jnp.int32),
                pltpu.VMEM((8, 128), jnp.int32),
                pltpu.SMEM((8, 128), jnp.int32),
                pltpu.VMEM((n_tm, 8, 128), jnp.int32),
                pltpu.VMEM((3, rows + 2, 2, half, columns), BF16),
                pltpu.VMEM((384, 1152), BF16),
                pltpu.VMEM((384, 768), BF16),
                pltpu.VMEM((rows, 384, columns), F32),
                pltpu.VMEM((2, rows, CHANNELS, columns), BF16),
                pltpu.VMEM((8, 128), F32),
                pltpu.VMEM((total, 8, 128), F32),
                pltpu.SMEM((n_tm, 8, 128), jnp.int32),
                pltpu.VMEM((2, 2, lat_rows, moments // 2, columns // 2), BF16),
                pltpu.VMEM((n_tm * frames_here * lat_rows, moments // 2, columns // 2), BF16),
                pltpu.VMEM((2, CHANNELS, columns // 2), F32),
                pltpu.SemaphoreType.REGULAR((2,)),
                dma((2,)),
                dma((rows,)),
                dma((2,)),
                dma((2,)),
                dma((2,)),
                dma((2,)),
                dma((1,)),
                dma((1,)),
                dma((2,)),
                dma((2,)),
                dma((1,)),
                dma((1,)),
                dma((1,)),
                dma((1,)),
                dma((2,)),
                dma((1,)),
                dma((9,)),
            ],
            compiler_params=pltpu.CompilerParams(
                collective_id=0, has_side_effects=True, vmem_limit_bytes=24 * 1024 * 1024
            ),
        )(*(
            pltpu.with_memory_space_constraint(operand, pltpu.HBM)
            for operand in (
                frame_clip.reshape(1, -1), owner.reshape(1, -1), activations, conv_weight,
                norm_gain.reshape(1, -1), norm_bias.reshape(1, -1),
                out_weight.transpose(0, 1, 3, 2).reshape(4, moments, CHANNELS),
            )
        ))

    placed = (
        P(("groups", "chan"), "tm", "space", None),
        P(("groups", "tm")),
        P(),
        P(),
        P(),
        P(),
        P(("groups", "space"), "tm", None),
    )
    return jax.shard_map(
        shards,
        mesh=mesh,
        in_specs=placed,
        out_specs=P(("groups", "space"), "tm", "chan", None),
        check_vma=False,
    )
```

```python
import functools

import jax
import jax.numpy as jnp
from jax import lax
from jax.experimental import pallas as pl
from jax.experimental.pallas import tpu as pltpu
from jax.sharding import PartitionSpec as P

CHANNELS = 128
GROUPS = 32
GROUP_SIZE = CHANNELS // GROUPS
F32 = jnp.float32
BF16 = jnp.bfloat16
MESH = pl.DeviceIdType.MESH


def kernel(
    sizes, clip_hbm, owner_hbm, act_in, weight_in, gain_in, bias_in, out_weight_in, out,
    clip_in, owner_in, act_raw, weight, gain, bias, out_weight, meta_in, near_meta, near_ids, meta,
    x, wt, wz, acc, conv, stat, stats, ids, latent, arrived, sums,
    round_sem, z_send, z_recv, edge_send, edge_recv, fwd_send, fwd_recv, peer_send, peer_recv,
    meta_send, meta_recv, owner_send, owner_recv, stat_send, stat_recv, lat_send, lat_recv, local_sem,
):
    n_tm, n_space, capacity = sizes
    half, frames_here, rows, columns = act_raw.shape
    lanes = columns // 2
    total = n_tm * n_space * 2
    n_frames = n_tm * frames_here
    lat_rows = rows // 2
    own_rows = frames_here * lat_rows
    piece_rows = lat_rows // 2
    half_rows = rows // 2
    t = lax.axis_index("tm")
    s = lax.axis_index("space")
    c = lax.axis_index("chan")
    me = (t * n_space + s) * 2 + c
    first = t == 0
    has_main = jnp.logical_or(c == 1, t < n_tm - 1)
    mirror = n_space == 2
    flip = s == 0 if mirror else False
    rounds = max(n_tm // 2 + n_space - 1, n_tm - 1) - 1

    def repeat(count, body):
        if count <= 4:
            for n in range(count):
                body(n)
        else:
            pl.loop(0, count)(body)

    def row_of(p):
        return jnp.where(flip, rows - 1 - p, p) if mirror else p

    fetches = [
        pltpu.make_async_copy(source, held, local_sem.at[n])
        for n, (source, held) in enumerate((
            (act_in, act_raw), (clip_hbm, clip_in), (owner_hbm, owner_in), (weight_in, weight),
            (gain_in, gain), (bias_in, bias), (out_weight_in, out_weight),
        ))
    ]
    for fetch in fetches[:3]:
        fetch.start()
    stats[...] = jnp.full(stats.shape, -1.0, F32)
    stat[...] = jnp.full(stat.shape, -1.0, F32)

    up_ok, down_ok = t < n_tm - 1, t > 0
    low_ok, high_ok = s > 0, s < n_space - 1
    t_up, t_down = jnp.minimum(t + 1, n_tm - 1), jnp.maximum(t - 1, 0)
    s_low, s_high = jnp.maximum(s - 1, 0), jnp.minimum(s + 1, n_space - 1)
    around = [(up_ok, t_up, s), (down_ok, t_down, s), (low_ok, t, s_low), (high_ok, t, s_high)]
    near_count = jnp.int32(1)
    for ok, _, _ in around:
        near_count = near_count + jnp.where(ok, 2, 0)

    def greet(semaphore):
        for ok, tt, ss in around:
            @pl.when(ok)
            def _(tt=tt, ss=ss):
                for core in range(2):
                    pl.semaphore_signal(
                        semaphore, inc=1, device_id={"tm": tt, "space": ss, "chan": core},
                        device_id_type=MESH,
                    )
        pl.semaphore_signal(
            semaphore, inc=1, device_id={"tm": t, "space": s, "chan": 1 - c}, device_id_type=MESH
        )

    barrier = pltpu.get_barrier_semaphore()
    greet(barrier)

    zero_row = jnp.zeros((3, 2, half, columns), BF16)

    @pl.when(s == 0)
    def _():
        x[:, 0] = zero_row

    @pl.when(s == n_space - 1)
    def _():
        x[:, rows + 1] = zero_row

    @pl.when(jnp.logical_and(first, c == 1))
    def _():
        x[0] = jnp.zeros((rows + 2, 2, half, columns), BF16)

    fetches[1].wait()
    fetches[2].wait()
    place = lax.broadcasted_iota(jnp.int32, (8, 128), 1)
    numbers = jnp.zeros((8, 128), jnp.int32)
    for n in range(frames_here):
        numbers = jnp.where(place == n, clip_in[0, n], numbers)
    for n in range(own_rows):
        numbers = jnp.where(place == frames_here + n, owner_in[0, n], numbers)
    meta_in[...] = numbers
    meta[t] = numbers

    gets_z = jnp.logical_or(
        jnp.logical_and(c == 0, up_ok), jnp.logical_and(c == 1, down_ok)
    )

    @pl.when(jnp.logical_not(gets_z))
    def _():
        near_meta[...] = numbers

    split_row = lax.broadcasted_iota(jnp.int32, (columns, columns), 0)
    split_col = lax.broadcasted_iota(jnp.int32, (columns, columns), 1)
    picked = jnp.where(split_col < lanes, 2 * split_col, 2 * (split_col - lanes) + 1)
    split = jnp.where(split_row == picked, 1.0, 0.0).astype(BF16)

    fetches[0].wait()
    for fetch in fetches[3:]:
        fetch.start()
    for f in range(frames_here):
        turned = jnp.transpose(act_raw[:, f], (1, 0, 2)).reshape(rows * half, columns)
        x[c + f, pl.ds(1, rows), c] = jnp.dot(
            turned, split, preferred_element_type=F32
        ).astype(BF16).reshape(rows, half, columns)

    pl.semaphore_wait(barrier, near_count)

    def remote(src, dst, send, recv, device):
        return pltpu.make_async_remote_copy(
            src_ref=src, dst_ref=dst, send_sem=send, recv_sem=recv, device_id=device,
            device_id_type=MESH,
        )

    groups = ((0, 1), (1, rows - 3), (rows - 2, 2))

    def z_copy(up, group):
        p, count = groups[group]
        frame, slot, core, tt = (1, 0, 1, t_up) if up else (0, 2, 0, t_down)
        begin = 1 + (jnp.where(flip, rows - p - count, p) if mirror else p)
        return remote(
            x.at[c + frame, pl.ds(begin, count), c], x.at[slot, pl.ds(begin, count), c],
            z_send.at[int(up)], z_recv.at[group], {"tm": tt, "space": s, "chan": core},
        )

    meta_copy = remote(
        meta_in, near_meta, meta_send.at[0], meta_recv.at[0],
        {"tm": jnp.where(c == 0, t_down, t_up), "space": s, "chan": c},
    )
    meta_sent = jnp.logical_or(
        jnp.logical_and(c == 0, down_ok), jnp.logical_and(c == 1, up_ok)
    )

    def edge(low, core):
        return remote(
            x.at[pl.ds(c, 2), 1 if low else rows, c],
            x.at[pl.ds(core, 2), rows + 1 if low else 0, c],
            edge_send.at[int(low)], edge_recv.at[int(low)],
            {"tm": t, "space": s_low if low else s_high, "chan": core},
        )

    z_slot = 2 * (1 - c)

    def forward(low):
        return remote(
            x.at[z_slot, 1 if low else rows], x.at[z_slot, rows + 1 if low else 0],
            fwd_send.at[int(low)], fwd_recv.at[int(low)],
            {"tm": t, "space": s_low if low else s_high, "chan": c},
        )

    peer = remote(
        x.at[pl.ds(c, 2), pl.ds(1, rows), c], x.at[pl.ds(1 - c, 2), pl.ds(1, rows), c],
        peer_send.at[0], peer_recv.at[0], {"tm": t, "space": s, "chan": 1 - c},
    )
    zs = ((True, up_ok), (False, down_ok))
    sides = ((True, low_ok), (False, high_ok))

    def start_z(group):
        for up, ok in zs:
            @pl.when(ok)
            def _(up=up):
                z_copy(up, group).start()

    @pl.when(meta_sent)
    def _():
        meta_copy.start()

    peer.start()
    start_z(0)
    for low, ok in sides:
        @pl.when(ok)
        def _(low=low):
            edge(low, 0).start()
            edge(low, 1).start()
    start_z(1)
    start_z(2)

    if rounds > 0:
        greet(round_sem.at[0])

    fetches[3].wait()
    for k in range(3):
        for i in range(3):
            for j in range(3):
                wt[pl.ds(j * 128, 128), pl.ds((3 * k + i) * 128, 128)] = weight[k, i, j].T
    for fetch in fetches[4:]:
        fetch.wait()

    peer.wait_recv()
    if rounds > 0:
        pl.semaphore_wait(round_sem.at[0], near_count)

        @pl.loop(1, rounds)
        def _(r):
            greet(round_sem.at[lax.rem(r, 2)])

            @pl.when(r < rounds - 1)
            def _():
                pl.semaphore_wait(round_sem.at[lax.rem(r, 2)], near_count)

    lane = lax.broadcasted_iota(jnp.int32, (CHANNELS, lanes), 1)

    def own_taps(h):
        return jnp.dot(
            wt[...], jnp.concatenate([tap(h) for tap in taps_of_own], axis=0),
            preferred_element_type=F32,
        )

    def first_frame(h):
        seen = slab(c)(h)
        return jnp.dot(
            wt[...], jnp.concatenate([seen] * 3, axis=0), preferred_element_type=F32
        )

    def with_z(h):
        seen = slab(z_slot)(h)
        return acc[h] + jnp.dot(wz[...], seen, preferred_element_type=F32)

    def conv_row(h, kept, summed):
        found = summed(h)
        even, odd = found[:, :lanes], found[:, lanes:]
        before = jnp.where(lane == 0, 0.0, pltpu.roll(odd[0:128], 1, 1))
        after = jnp.where(lane == lanes - 1, 0.0, pltpu.roll(even[256:384], lanes - 1, 1))
        even, odd = (
            (before + even[128:256] + odd[256:384]).astype(BF16),
            (even[0:128] + odd[128:256] + after).astype(BF16),
        )
        conv[kept, h] = jnp.concatenate([even, odd], axis=1)
        a, b = even.astype(F32), odd.astype(F32)
        return a + b, a * a + b * b

    def conv_rows(places, kept, summed):
        found = [conv_row(h, kept, summed) for h in places]
        for q in range(2):
            total_q = found[0][q]
            for one in found[1:]:
                total_q = total_q + one[q]
            sums[q] += total_q

    def slab(slot):
        return lambda h: x[slot, pl.ds(h, 3)].reshape(3 * CHANNELS, columns)

    def sums_to(row):
        stat[pl.ds(row, 1), :] = jnp.sum(sums[0].T, axis=0, keepdims=True)
        stat[pl.ds(row + 1, 1), :] = jnp.sum(sums[1].T, axis=0, keepdims=True)

    def wait_edges():
        for low, ok in ((True, high_ok), (False, low_ok)):
            @pl.when(ok)
            def _(low=low):
                there = x.at[pl.ds(c, 2), rows + 1 if low else 0]
                remote(
                    there, there, edge_send.at[int(low)], edge_recv.at[int(low)],
                    {"tm": t, "space": s, "chan": c},
                ).wait_recv()

    def wait_z(group):
        p, count = groups[group]

        @pl.when(gets_z)
        def _():
            begin = 1 + (jnp.where(flip, rows - p - count, p) if mirror else p)
            there = x.at[z_slot, pl.ds(begin, count)]
            remote(
                there, there, z_send.at[0], z_recv.at[group], {"tm": t, "space": s, "chan": c}
            ).wait_recv()

    def start_forwards():
        for low, ok in sides:
            @pl.when(jnp.logical_and(gets_z, ok))
            def _(low=low):
                forward(low).start()

    def wait_forwards():
        for low, ok in ((True, high_ok), (False, low_ok)):
            @pl.when(jnp.logical_and(gets_z, ok))
            def _(low=low):
                forward(low).wait_recv()

    half_index = jnp.where(flip, c, 1 - c) if mirror else c

    if not mirror:
        wait_edges()

    @pl.when(first)
    def _():
        sums[...] = jnp.zeros_like(sums)

        if mirror:
            @pl.when(c == 1)
            def _():
                wait_edges()
        begin = jnp.where(c == 0, half_rows, 0) if mirror else c * half_rows
        conv_rows(
            [row_of(begin + p) for p in range(half_rows - 1, -1, -1)], 1, first_frame
        )
        sums_to(3)

    @pl.when(gets_z)
    def _():
        meta_copy.wait_recv()

    to_scalars = pltpu.make_async_copy(near_meta, near_ids, local_sem.at[7])
    to_scalars.start()
    to_scalars.wait()

    my_clip = jnp.where(c == 1, clip_in[0, 1], near_ids[0, 0])
    newer = jnp.where(c == 1, clip_in[0, 0], clip_in[0, 1]) == my_clip
    older = jnp.logical_and(
        jnp.logical_or(c == 0, t > 0),
        jnp.where(c == 1, near_ids[0, 1], clip_in[0, 0]) == my_clip,
    )

    w_old, w_mid, w_new = (
        wt[:, pl.ds(k * 3 * CHANNELS, 3 * CHANNELS)].astype(F32) for k in range(3)
    )
    on_z = jnp.where(
        c == 0, w_new + jnp.where(newer, 0.0, w_mid + w_old), jnp.where(older, w_old, 0.0)
    )
    wz[...] = on_z.astype(BF16)

    row8 = lax.broadcasted_iota(jnp.int32, (8, 128), 0)
    lane8 = lax.broadcasted_iota(jnp.int32, (8, 128), 1)
    facts = jnp.where(row8 == 2, jnp.where(has_main, my_clip, -1).astype(F32), -1.0)
    facts = jnp.where(
        jnp.logical_and(row8 == 5, first), clip_in[0, 0].astype(F32), facts
    )
    stat[pl.ds(2, 1), :] = facts[2:3]
    stat[pl.ds(5, 1), :] = facts[5:6]

    none = jnp.zeros((3 * CHANNELS, columns), BF16)

    def newest(h):
        return jnp.where(c == 1, slab(1 + c)(h), none)

    def middle(h):
        return jnp.where(newer, slab(1)(h), newest(h))

    def oldest(h):
        return jnp.where(older, jnp.where(c == 0, slab(c)(h), none), middle(h))

    taps_of_own = [oldest, middle, newest]

    def own_rows_of(places):
        for p in places:
            h = row_of(p)
            acc[h] = own_taps(h)

    steps = rows // 2

    def send_owners():
        def to(n):
            remote(
                meta_in, meta.at[t], owner_send.at[0], owner_recv.at[0],
                {"tm": lax.rem(t + 1 + n, n_tm), "space": s, "chan": c},
            ).start()

        repeat(n_tm - 1, to)

    def owner_wait(received):
        span = meta.at[pl.ds(0, n_tm - 1)]
        copy = remote(
            span, span, owner_send.at[0], owner_recv.at[0], {"tm": t, "space": s, "chan": c}
        )
        copy.wait_recv() if received else copy.wait_send()

    tail = (rows - 3, 0, rows - 2, rows - 1)

    @pl.when(has_main)
    def _():
        own_rows_of(range(1, rows - 3))

    if mirror:
        wait_z(0)
        start_forwards()

        @pl.when(jnp.logical_not(jnp.logical_and(first, c == 1)))
        def _():
            wait_edges()
    else:
        for group in range(3):
            wait_z(group)
        start_forwards()
        wait_forwards()

    @pl.when(has_main)
    def _():
        own_rows_of(tail)

    sums[...] = jnp.zeros_like(sums)

    if mirror:
        wait_z(1)

    @pl.when(has_main)
    def _():
        conv_rows([row_of(p) for p in range(1, rows - 3)], 0, with_z)

    if mirror:
        wait_forwards()
        wait_z(2)

    @pl.when(has_main)
    def _():
        conv_rows([row_of(p) for p in tail], 0, with_z)

    @pl.when(has_main)
    def _():
        sums_to(0)

    stats[me] = stat[...]
    if rounds > 1:
        pl.semaphore_wait(round_sem.at[(rounds - 1) % 2], near_count)

    def stat_copy(tt, ss, core):
        return remote(
            stat, stats.at[me], stat_send.at[0], stat_recv.at[0],
            {"tm": tt, "space": ss, "chan": core},
        )

    reach = n_tm // 2

    def spaces(act):
        repeat(n_space, lambda n: act(lax.rem(s + n_space - 1 - n, n_space), n))

    far_t = jnp.where(c == 0, t + reach, t - reach)

    @pl.when(jnp.logical_and(far_t >= 0, far_t < n_tm))
    def _():
        spaces(lambda ss, n: stat_copy(far_t, ss, 1 - c).start())

    def slab_both(away):
        for tt in (t + away, t - away):
            @pl.when(jnp.logical_and(tt >= 0, tt < n_tm))
            def _(tt=tt):
                for core in range(2):
                    spaces(lambda ss, n: stat_copy(tt, ss, core).start())

    repeat(reach - 1, lambda n: slab_both(reach - 1 - n))
    repeat(n_space - 1, lambda n: [
        stat_copy(t, lax.rem(s + 1 + n, n_space), core).start() for core in range(2)
    ] and None)
    stat_copy(t, s, 1 - c).start()
    send_owners()

    stat_counts = {
        (tt, core): 2 * n_space - 1 + sum(
            n_space * len([o for o in (0, 1) if abs(2 * (other - tt) + core - o) < n_tm])
            for other in range(n_tm) if other != tt
        )
        for tt in range(n_tm) for core in range(2)
    }

    def stat_wait(received):
        for count in sorted(set(stat_counts.values())):
            same = False
            for (tt, core), number in stat_counts.items():
                if number == count:
                    same = jnp.logical_or(same, jnp.logical_and(t == tt, c == core))

            @pl.when(same)
            def _(count=count):
                span = stats.at[pl.ds(0, count)]
                copy = remote(
                    span, span, stat_send.at[0], stat_recv.at[0],
                    {"tm": t, "space": s, "chan": c},
                )
                copy.wait_recv() if received else copy.wait_send()

    weights = jnp.concatenate([out_weight[q] for q in range(4)], axis=1)

    stat_wait(True)

    sizes_row = jnp.where(
        row8 == 2, float(rows * columns), float(half_rows * columns)
    )
    is_size = jnp.logical_or(row8 == 2, row8 == 5)

    def add_source(source, carry, clip):
        value = stats[source]
        key = jnp.where(row8 < 3, value[2:3], value[5:6])
        value = jnp.where(is_size, sizes_row, value)
        return carry + jnp.where(key == clip, value, 0.0)

    def moments_of(clip):
        clip = clip.astype(F32)
        found = jnp.zeros((8, 128), F32)
        if total <= 32:
            for source in range(total):
                found = add_source(source, found, clip)
        else:
            found = lax.fori_loop(
                0, total, lambda source, carry: add_source(source, carry, clip), found
            )
        found = found + pltpu.roll(found, 5, 0)
        found = found + jnp.where(
            lane8 % 2 == 0, pltpu.roll(found, 127, 1), pltpu.roll(found, 1, 1)
        )
        found = found + jnp.where(
            lane8 % 4 < 2, pltpu.roll(found, 126, 1), pltpu.roll(found, 2, 1)
        )
        count = found[2:3]
        mean = found[0:1] / count
        var = found[1:2] / count - mean * mean
        scale = lax.rsqrt(var + 1e-6) * gain[...] * 0.5
        shift = bias[...] * 0.5 - mean * scale
        return jnp.broadcast_to(scale, (128, 128)).T, jnp.broadcast_to(shift, (128, 128)).T

    def finish(kept, begin, count, scale_c, shift_c):
        wide = []
        for r in range(count):
            pieces = []
            for i in range(2):
                value = conv[kept, 2 * (begin + r) + i].astype(F32)
                for j in range(2):
                    v = value[:, j * lanes:(j + 1) * lanes] * scale_c + shift_c
                    pieces.append((v + v * jnp.tanh(v)).astype(BF16))
            wide.append(jnp.concatenate(pieces, axis=0))
        result = jnp.dot(
            weights, jnp.concatenate(wide, axis=1), preferred_element_type=F32
        ).astype(BF16)
        for r in range(count):
            for core in range(2):
                latent[kept, core, begin + r] = result[
                    core * 16:core * 16 + 16, r * lanes:(r + 1) * lanes
                ]

    def send_latent(kept, begin, count, frame):
        span = pl.ds(frame * lat_rows + begin, count)
        arrived[span] = latent[kept, c, pl.ds(begin, count)]

        def to(tt, core):
            remote(
                latent.at[kept, core, pl.ds(begin, count)], arrived.at[span],
                lat_send.at[kept], lat_recv.at[0], {"tm": tt, "space": s, "chan": core},
            ).start()

        def others(n):
            step = jnp.where(t < n_tm // 2, n_tm - 1 - n, 1 + n)
            for core in range(2):
                to(lax.rem(t + step, n_tm), core)

        repeat(n_tm - 1, others)
        to(t, 1 - c)

    my_frame = 2 * t + 2 - c

    @pl.when(first)
    def _():
        finish(1, half_index * piece_rows, piece_rows, *moments_of(clip_in[0, 0]))
        send_latent(1, half_index * piece_rows, piece_rows, 0)

    @pl.when(has_main)
    def _():
        found = moments_of(my_clip)
        finish(0, 0, lat_rows, *found)
        send_latent(0, 0, lat_rows, my_frame)

    owner_wait(True)
    owners = pltpu.make_async_copy(meta, ids, local_sem.at[8])
    owners.start()
    owners.wait()

    def arrived_wait(count):
        span = arrived.at[pl.ds(0, count)]
        remote(
            span, span, lat_send.at[0], lat_recv.at[0], {"tm": t, "space": s, "chan": c}
        ).wait_recv()

    every = n_frames * lat_rows

    @pl.when(first)
    def _():
        arrived_wait(every - lat_rows - piece_rows)

    @pl.when(jnp.logical_and(has_main, t > 0))
    def _():
        arrived_wait(every - lat_rows)

    @pl.when(jnp.logical_not(has_main))
    def _():
        arrived_wait(every)

    @pl.loop(0, n_tm)
    def _(b):
        taken = jnp.int32(0)
        slots = []
        for n in range(own_rows):
            hit = ids[b, 0, frames_here + n] == t
            slots.append(jnp.where(hit, taken, -1))
            taken = taken + jnp.where(hit, 1, 0)
        for j in range(capacity):
            value = jnp.zeros((16, lanes), BF16)
            for n in range(own_rows):
                value = jnp.where(slots[n] == j, arrived[b * own_rows + n], value)
            out[0, b * capacity + j] = value

    peer.wait_send()
    for up, ok in zs:
        @pl.when(ok)
        def _(up=up):
            span = x.at[0, pl.ds(1, rows), 0]
            remote(
                span, span, z_send.at[int(up)], z_recv.at[0],
                {"tm": t, "space": s, "chan": c},
            ).wait_send()
    for low, ok in sides:
        @pl.when(ok)
        def _(low=low):
            there = x.at[pl.ds(0, 2), 0]
            remote(
                there, there, edge_send.at[int(low)], edge_recv.at[int(low)],
                {"tm": t, "space": s, "chan": c},
            ).wait_send()

            @pl.when(gets_z)
            def _():
                forward(low).wait_send()

    @pl.when(meta_sent)
    def _():
        meta_copy.wait_send()

    stat_wait(False)
    owner_wait(False)

    def latents_left(kept, count):
        span = arrived.at[pl.ds(0, count)]
        remote(
            span, span, lat_send.at[kept], lat_recv.at[0], {"tm": t, "space": s, "chan": c}
        ).wait_send()

    @pl.when(first)
    def _():
        latents_left(1, (2 * n_tm - 1) * piece_rows)

    @pl.when(has_main)
    def _():
        latents_left(0, (2 * n_tm - 1) * lat_rows)


def solution(mesh):
    n_tm, n_space = mesh.shape["tm"], mesh.shape["space"]
    total = n_tm * n_space * 2

    def shards(activations, frame_clip, conv_weight, norm_gain, norm_bias, out_weight, owner):
        half, frames_here, rows, columns = activations.shape
        lat_rows = rows // 2
        capacity = max(2, 2 * frames_here * lat_rows // n_tm)
        moments = out_weight.shape[-1]
        dma = pltpu.SemaphoreType.DMA
        return pl.pallas_call(
            functools.partial(kernel, (n_tm, n_space, capacity)),
            out_shape=jax.ShapeDtypeStruct(
                (1, n_tm * capacity, moments // 2, columns // 2), BF16
            ),
            in_specs=[pl.BlockSpec(memory_space=pltpu.HBM)] * 7,
            out_specs=pl.BlockSpec(memory_space=pltpu.VMEM),
            scratch_shapes=[
                pltpu.SMEM((1, frames_here), jnp.int32),
                pltpu.SMEM((1, frames_here * lat_rows), jnp.int32),
                pltpu.VMEM(activations.shape, BF16),
                pltpu.VMEM(conv_weight.shape, BF16),
                pltpu.VMEM((1, CHANNELS), F32),
                pltpu.VMEM((1, CHANNELS), F32),
                pltpu.VMEM((4, moments, CHANNELS), BF16),
                pltpu.VMEM((8, 128), jnp.int32),
                pltpu.VMEM((8, 128), jnp.int32),
                pltpu.SMEM((8, 128), jnp.int32),
                pltpu.VMEM((n_tm, 8, 128), jnp.int32),
                pltpu.VMEM((3, rows + 2, 2, half, columns), BF16),
                pltpu.VMEM((384, 1152), BF16),
                pltpu.VMEM((384, 384), BF16),
                pltpu.VMEM((rows, 384, columns), F32),
                pltpu.VMEM((2, rows, CHANNELS, columns), BF16),
                pltpu.VMEM((8, 128), F32),
                pltpu.VMEM((total, 8, 128), F32),
                pltpu.SMEM((n_tm, 8, 128), jnp.int32),
                pltpu.VMEM((2, 2, lat_rows, moments // 2, columns // 2), BF16),
                pltpu.VMEM((n_tm * frames_here * lat_rows, moments // 2, columns // 2), BF16),
                pltpu.VMEM((2, CHANNELS, columns // 2), F32),
                pltpu.SemaphoreType.REGULAR((2,)),
                dma((2,)),
                dma((3,)),
                dma((2,)),
                dma((2,)),
                dma((2,)),
                dma((2,)),
                dma((1,)),
                dma((1,)),
                dma((2,)),
                dma((2,)),
                dma((1,)),
                dma((1,)),
                dma((1,)),
                dma((1,)),
                dma((2,)),
                dma((1,)),
                dma((9,)),
            ],
            compiler_params=pltpu.CompilerParams(
                collective_id=0, has_side_effects=True, vmem_limit_bytes=24 * 1024 * 1024
            ),
        )(*(
            pltpu.with_memory_space_constraint(operand, pltpu.HBM)
            for operand in (
                frame_clip.reshape(1, -1), owner.reshape(1, -1), activations, conv_weight,
                norm_gain.reshape(1, -1), norm_bias.reshape(1, -1),
                out_weight.transpose(0, 1, 3, 2).reshape(4, moments, CHANNELS),
            )
        ))

    placed = (
        P(("groups", "chan"), "tm", "space", None),
        P(("groups", "tm")),
        P(),
        P(),
        P(),
        P(),
        P(("groups", "space"), "tm", None),
    )
    return jax.shard_map(
        shards,
        mesh=mesh,
        in_specs=placed,
        out_specs=P(("groups", "space"), "tm", "chan", None),
        check_vma=False,
    )
```

```python
import functools

import jax
import jax.numpy as jnp
from jax import lax
from jax.experimental import pallas as pl
from jax.experimental.pallas import tpu as pltpu
from jax.sharding import PartitionSpec as P

CHANNELS = 128
GROUPS = 32
GROUP_SIZE = CHANNELS // GROUPS
F32 = jnp.float32
BF16 = jnp.bfloat16
MESH = pl.DeviceIdType.MESH


def kernel(
    sizes, clip_hbm, owner_hbm, act_in, weight_in, gain_in, bias_in, out_weight_in, out,
    clip_in, owner_in, act_raw, weight, gain, bias, out_weight, meta_in, near_meta, near_ids, meta,
    x, wt, wz, acc, conv, stat, stats, ids, latent, arrived, sums,
    round_sem, z_send, z_recv, edge_send, edge_recv, fwd_send, fwd_recv, peer_send, peer_recv,
    meta_send, meta_recv, owner_send, owner_recv, stat_send, stat_recv, lat_send, lat_recv, local_sem,
):
    n_tm, n_space, capacity = sizes
    half, frames_here, rows, columns = act_raw.shape
    lanes = columns // 2
    total = n_tm * n_space * 2
    n_frames = n_tm * frames_here
    lat_rows = rows // 2
    own_rows = frames_here * lat_rows
    piece_rows = lat_rows // 2
    half_rows = rows // 2
    t = lax.axis_index("tm")
    s = lax.axis_index("space")
    c = lax.axis_index("chan")
    me = (t * n_space + s) * 2 + c
    first = t == 0
    has_main = jnp.logical_or(c == 1, t < n_tm - 1)
    mirror = n_space == 2
    flip = s == 0 if mirror else False
    rounds = max(n_tm // 2 + n_space - 1, n_tm - 1) - 1

    def repeat(count, body):
        if count <= 4:
            for n in range(count):
                body(n)
        else:
            pl.loop(0, count)(body)

    def row_of(p):
        return jnp.where(flip, rows - 1 - p, p) if mirror else p

    fetches = [
        pltpu.make_async_copy(source, held, local_sem.at[n])
        for n, (source, held) in enumerate((
            (act_in, act_raw), (clip_hbm, clip_in), (owner_hbm, owner_in), (weight_in, weight),
            (gain_in, gain), (bias_in, bias), (out_weight_in, out_weight),
        ))
    ]
    for fetch in fetches[:3]:
        fetch.start()
    stats[...] = jnp.full(stats.shape, -1.0, F32)
    stat[...] = jnp.full(stat.shape, -1.0, F32)

    up_ok, down_ok = t < n_tm - 1, t > 0
    low_ok, high_ok = s > 0, s < n_space - 1
    t_up, t_down = jnp.minimum(t + 1, n_tm - 1), jnp.maximum(t - 1, 0)
    s_low, s_high = jnp.maximum(s - 1, 0), jnp.minimum(s + 1, n_space - 1)
    around = [(up_ok, t_up, s), (down_ok, t_down, s), (low_ok, t, s_low), (high_ok, t, s_high)]
    near_count = jnp.int32(1)
    for ok, _, _ in around:
        near_count = near_count + jnp.where(ok, 2, 0)

    def greet(semaphore):
        for ok, tt, ss in around:
            @pl.when(ok)
            def _(tt=tt, ss=ss):
                for core in range(2):
                    pl.semaphore_signal(
                        semaphore, inc=1, device_id={"tm": tt, "space": ss, "chan": core},
                        device_id_type=MESH,
                    )
        pl.semaphore_signal(
            semaphore, inc=1, device_id={"tm": t, "space": s, "chan": 1 - c}, device_id_type=MESH
        )

    barrier = pltpu.get_barrier_semaphore()
    greet(barrier)

    zero_row = jnp.zeros((3, 2, half, columns), BF16)

    @pl.when(s == 0)
    def _():
        x[:, 0] = zero_row

    @pl.when(s == n_space - 1)
    def _():
        x[:, rows + 1] = zero_row

    @pl.when(jnp.logical_and(first, c == 1))
    def _():
        x[0] = jnp.zeros((rows + 2, 2, half, columns), BF16)

    fetches[1].wait()
    fetches[2].wait()
    place = lax.broadcasted_iota(jnp.int32, (8, 128), 1)
    numbers = jnp.zeros((8, 128), jnp.int32)
    for n in range(frames_here):
        numbers = jnp.where(place == n, clip_in[0, n], numbers)
    for n in range(own_rows):
        numbers = jnp.where(place == frames_here + n, owner_in[0, n], numbers)
    meta_in[...] = numbers
    meta[t] = numbers

    gets_z = jnp.logical_or(
        jnp.logical_and(c == 0, up_ok), jnp.logical_and(c == 1, down_ok)
    )

    @pl.when(jnp.logical_not(gets_z))
    def _():
        near_meta[...] = numbers

    split_row = lax.broadcasted_iota(jnp.int32, (columns, columns), 0)
    split_col = lax.broadcasted_iota(jnp.int32, (columns, columns), 1)
    picked = jnp.where(split_col < lanes, 2 * split_col, 2 * (split_col - lanes) + 1)
    split = jnp.where(split_row == picked, 1.0, 0.0).astype(BF16)

    fetches[0].wait()
    for fetch in fetches[3:]:
        fetch.start()
    for f in range(frames_here):
        turned = jnp.transpose(act_raw[:, f], (1, 0, 2)).reshape(rows * half, columns)
        x[c + f, pl.ds(1, rows), c] = jnp.dot(
            turned, split, preferred_element_type=F32
        ).astype(BF16).reshape(rows, half, columns)

    pl.semaphore_wait(barrier, near_count)

    def remote(src, dst, send, recv, device):
        return pltpu.make_async_remote_copy(
            src_ref=src, dst_ref=dst, send_sem=send, recv_sem=recv, device_id=device,
            device_id_type=MESH,
        )

    groups = ((0, 1), (1, rows - 3), (rows - 2, 2))

    def z_copy(up, group):
        p, count = groups[group]
        frame, slot, core, tt = (1, 0, 1, t_up) if up else (0, 2, 0, t_down)
        begin = 1 + (jnp.where(flip, rows - p - count, p) if mirror else p)
        return remote(
            x.at[c + frame, pl.ds(begin, count), c], x.at[slot, pl.ds(begin, count), c],
            z_send.at[int(up)], z_recv.at[group], {"tm": tt, "space": s, "chan": core},
        )

    meta_copy = remote(
        meta_in, near_meta, meta_send.at[0], meta_recv.at[0],
        {"tm": jnp.where(c == 0, t_down, t_up), "space": s, "chan": c},
    )
    meta_sent = jnp.logical_or(
        jnp.logical_and(c == 0, down_ok), jnp.logical_and(c == 1, up_ok)
    )

    def edge(low, core):
        return remote(
            x.at[pl.ds(c, 2), 1 if low else rows, c],
            x.at[pl.ds(core, 2), rows + 1 if low else 0, c],
            edge_send.at[int(low)], edge_recv.at[int(low)],
            {"tm": t, "space": s_low if low else s_high, "chan": core},
        )

    z_slot = 2 * (1 - c)

    def forward(low):
        return remote(
            x.at[z_slot, 1 if low else rows], x.at[z_slot, rows + 1 if low else 0],
            fwd_send.at[int(low)], fwd_recv.at[int(low)],
            {"tm": t, "space": s_low if low else s_high, "chan": c},
        )

    peer = remote(
        x.at[pl.ds(c, 2), pl.ds(1, rows), c], x.at[pl.ds(1 - c, 2), pl.ds(1, rows), c],
        peer_send.at[0], peer_recv.at[0], {"tm": t, "space": s, "chan": 1 - c},
    )
    zs = ((True, up_ok), (False, down_ok))
    sides = ((True, low_ok), (False, high_ok))

    def start_z(group):
        for up, ok in zs:
            @pl.when(ok)
            def _(up=up):
                z_copy(up, group).start()

    @pl.when(meta_sent)
    def _():
        meta_copy.start()

    peer.start()
    start_z(0)
    for low, ok in sides:
        @pl.when(ok)
        def _(low=low):
            edge(low, 0).start()
            edge(low, 1).start()
    start_z(1)
    start_z(2)

    if rounds > 0:
        greet(round_sem.at[0])

    fetches[3].wait()
    for k in range(3):
        for i in range(3):
            for j in range(3):
                wt[pl.ds(j * 128, 128), pl.ds((3 * k + i) * 128, 128)] = weight[k, i, j].T
    for fetch in fetches[4:]:
        fetch.wait()

    peer.wait_recv()
    if rounds > 0:
        pl.semaphore_wait(round_sem.at[0], near_count)

        @pl.loop(1, rounds)
        def _(r):
            greet(round_sem.at[lax.rem(r, 2)])

            @pl.when(r < rounds - 1)
            def _():
                pl.semaphore_wait(round_sem.at[lax.rem(r, 2)], near_count)

    lane = lax.broadcasted_iota(jnp.int32, (CHANNELS, lanes), 1)

    def own_taps(h):
        return jnp.dot(
            wt[...], jnp.concatenate([tap(h) for tap in taps_of_own], axis=0),
            preferred_element_type=F32,
        )

    def first_frame(h):
        seen = slab(c)(h)
        return jnp.dot(
            wt[...], jnp.concatenate([seen] * 3, axis=0), preferred_element_type=F32
        )

    def with_z(h):
        seen = slab(z_slot)(h)
        return acc[h] + jnp.dot(wz[...], seen, preferred_element_type=F32)

    def conv_row(h, kept, summed):
        found = summed(h)
        even, odd = found[:, :lanes], found[:, lanes:]
        before = jnp.where(lane == 0, 0.0, pltpu.roll(odd[0:128], 1, 1))
        after = jnp.where(lane == lanes - 1, 0.0, pltpu.roll(even[256:384], lanes - 1, 1))
        even, odd = (
            (before + even[128:256] + odd[256:384]).astype(BF16),
            (even[0:128] + odd[128:256] + after).astype(BF16),
        )
        conv[kept, h] = jnp.concatenate([even, odd], axis=1)
        a, b = even.astype(F32), odd.astype(F32)
        return a + b, a * a + b * b

    def conv_rows(places, kept, summed):
        found = [conv_row(h, kept, summed) for h in places]
        for q in range(2):
            total_q = found[0][q]
            for one in found[1:]:
                total_q = total_q + one[q]
            sums[q] += total_q

    def slab(slot):
        return lambda h: x[slot, pl.ds(h, 3)].reshape(3 * CHANNELS, columns)

    def sums_to(row):
        stat[pl.ds(row, 1), :] = jnp.sum(sums[0].T, axis=0, keepdims=True)
        stat[pl.ds(row + 1, 1), :] = jnp.sum(sums[1].T, axis=0, keepdims=True)

    def wait_edges():
        for low, ok in ((True, high_ok), (False, low_ok)):
            @pl.when(ok)
            def _(low=low):
                there = x.at[pl.ds(c, 2), rows + 1 if low else 0]
                remote(
                    there, there, edge_send.at[int(low)], edge_recv.at[int(low)],
                    {"tm": t, "space": s, "chan": c},
                ).wait_recv()

    def wait_z(group):
        p, count = groups[group]

        @pl.when(gets_z)
        def _():
            begin = 1 + (jnp.where(flip, rows - p - count, p) if mirror else p)
            there = x.at[z_slot, pl.ds(begin, count)]
            remote(
                there, there, z_send.at[0], z_recv.at[group], {"tm": t, "space": s, "chan": c}
            ).wait_recv()

    def start_forwards():
        for low, ok in sides:
            @pl.when(jnp.logical_and(gets_z, ok))
            def _(low=low):
                forward(low).start()

    def wait_forwards():
        for low, ok in ((True, high_ok), (False, low_ok)):
            @pl.when(jnp.logical_and(gets_z, ok))
            def _(low=low):
                forward(low).wait_recv()

    half_index = jnp.where(flip, c, 1 - c) if mirror else c

    if not mirror:
        wait_edges()

    @pl.when(first)
    def _():
        sums[...] = jnp.zeros_like(sums)

        if mirror:
            @pl.when(c == 1)
            def _():
                wait_edges()
        begin = jnp.where(c == 0, half_rows, 0) if mirror else c * half_rows
        conv_rows(
            [row_of(begin + p) for p in range(half_rows - 1, -1, -1)], 1, first_frame
        )
        sums_to(3)

    @pl.when(gets_z)
    def _():
        meta_copy.wait_recv()

    to_scalars = pltpu.make_async_copy(near_meta, near_ids, local_sem.at[7])
    to_scalars.start()
    to_scalars.wait()

    my_clip = jnp.where(c == 1, clip_in[0, 1], near_ids[0, 0])
    newer = jnp.where(c == 1, clip_in[0, 0], clip_in[0, 1]) == my_clip
    older = jnp.logical_and(
        jnp.logical_or(c == 0, t > 0),
        jnp.where(c == 1, near_ids[0, 1], clip_in[0, 0]) == my_clip,
    )

    w_old, w_mid, w_new = (
        wt[:, pl.ds(k * 3 * CHANNELS, 3 * CHANNELS)].astype(F32) for k in range(3)
    )
    on_z = jnp.where(
        c == 0, w_new + jnp.where(newer, 0.0, w_mid + w_old), jnp.where(older, w_old, 0.0)
    )
    wz[...] = on_z.astype(BF16)

    row8 = lax.broadcasted_iota(jnp.int32, (8, 128), 0)
    lane8 = lax.broadcasted_iota(jnp.int32, (8, 128), 1)
    facts = jnp.where(row8 == 2, jnp.where(has_main, my_clip, -1).astype(F32), -1.0)
    facts = jnp.where(
        jnp.logical_and(row8 == 5, first), clip_in[0, 0].astype(F32), facts
    )
    stat[pl.ds(2, 1), :] = facts[2:3]
    stat[pl.ds(5, 1), :] = facts[5:6]

    none = jnp.zeros((3 * CHANNELS, columns), BF16)

    def newest(h):
        return jnp.where(c == 1, slab(1 + c)(h), none)

    def middle(h):
        return jnp.where(newer, slab(1)(h), newest(h))

    def oldest(h):
        return jnp.where(older, jnp.where(c == 0, slab(c)(h), none), middle(h))

    taps_of_own = [oldest, middle, newest]

    def own_rows_of(places):
        for p in places:
            h = row_of(p)
            acc[h] = own_taps(h)

    steps = rows // 2

    def send_owners():
        def to(n):
            remote(
                meta_in, meta.at[t], owner_send.at[0], owner_recv.at[0],
                {"tm": lax.rem(t + 1 + n, n_tm), "space": s, "chan": c},
            ).start()

        repeat(n_tm - 1, to)

    def owner_wait(received):
        span = meta.at[pl.ds(0, n_tm - 1)]
        copy = remote(
            span, span, owner_send.at[0], owner_recv.at[0], {"tm": t, "space": s, "chan": c}
        )
        copy.wait_recv() if received else copy.wait_send()

    tail = (rows - 3, 0, rows - 2, rows - 1)

    @pl.when(has_main)
    def _():
        own_rows_of(range(1, rows - 3))

    if mirror:
        wait_z(0)
        start_forwards()

        @pl.when(jnp.logical_not(jnp.logical_and(first, c == 1)))
        def _():
            wait_edges()
    else:
        for group in range(3):
            wait_z(group)
        start_forwards()
        wait_forwards()

    @pl.when(has_main)
    def _():
        own_rows_of(tail)

    sums[...] = jnp.zeros_like(sums)

    if mirror:
        wait_z(1)

    @pl.when(has_main)
    def _():
        conv_rows([row_of(p) for p in range(1, rows - 3)], 0, with_z)

    if mirror:
        wait_forwards()
        wait_z(2)

    @pl.when(has_main)
    def _():
        conv_rows([row_of(p) for p in tail], 0, with_z)

    @pl.when(has_main)
    def _():
        sums_to(0)

    stats[me] = stat[...]
    if rounds > 1:
        pl.semaphore_wait(round_sem.at[(rounds - 1) % 2], near_count)

    def stat_copy(tt, ss, core):
        return remote(
            stat, stats.at[me], stat_send.at[0], stat_recv.at[0],
            {"tm": tt, "space": ss, "chan": core},
        )

    reach = n_tm // 2

    def spaces(act):
        repeat(n_space, lambda n: act(lax.rem(s + n_space - 1 - n, n_space), n))

    far_t = jnp.where(c == 0, t + reach, t - reach)

    @pl.when(jnp.logical_and(far_t >= 0, far_t < n_tm))
    def _():
        spaces(lambda ss, n: stat_copy(far_t, ss, 1 - c).start())

    def slab_both(away):
        for tt in (t + away, t - away):
            @pl.when(jnp.logical_and(tt >= 0, tt < n_tm))
            def _(tt=tt):
                for core in range(2):
                    spaces(lambda ss, n: stat_copy(tt, ss, core).start())

    repeat(reach - 1, lambda n: slab_both(reach - 1 - n))
    repeat(n_space - 1, lambda n: [
        stat_copy(t, lax.rem(s + 1 + n, n_space), core).start() for core in range(2)
    ] and None)
    stat_copy(t, s, 1 - c).start()
    send_owners()

    stat_counts = {
        (tt, core): 2 * n_space - 1 + sum(
            n_space * len([o for o in (0, 1) if abs(2 * (other - tt) + core - o) < n_tm])
            for other in range(n_tm) if other != tt
        )
        for tt in range(n_tm) for core in range(2)
    }

    def stat_wait(received):
        for count in sorted(set(stat_counts.values())):
            same = False
            for (tt, core), number in stat_counts.items():
                if number == count:
                    same = jnp.logical_or(same, jnp.logical_and(t == tt, c == core))

            @pl.when(same)
            def _(count=count):
                span = stats.at[pl.ds(0, count)]
                copy = remote(
                    span, span, stat_send.at[0], stat_recv.at[0],
                    {"tm": t, "space": s, "chan": c},
                )
                copy.wait_recv() if received else copy.wait_send()

    weights = jnp.concatenate([out_weight[q] for q in range(4)], axis=1)

    stat_wait(True)

    sizes_row = jnp.where(
        row8 == 2, float(rows * columns), float(half_rows * columns)
    )
    is_size = jnp.logical_or(row8 == 2, row8 == 5)

    def add_source(source, carry, clip):
        value = stats[source]
        key = jnp.where(row8 < 3, value[2:3], value[5:6])
        value = jnp.where(is_size, sizes_row, value)
        return carry + jnp.where(key == clip, value, 0.0)

    def moments_of(clip):
        clip = clip.astype(F32)
        found = jnp.zeros((8, 128), F32)
        if total <= 32:
            for source in range(total):
                found = add_source(source, found, clip)
        else:
            found = lax.fori_loop(
                0, total, lambda source, carry: add_source(source, carry, clip), found
            )
        found = found + pltpu.roll(found, 5, 0)
        found = found + jnp.where(
            lane8 % 2 == 0, pltpu.roll(found, 127, 1), pltpu.roll(found, 1, 1)
        )
        found = found + jnp.where(
            lane8 % 4 < 2, pltpu.roll(found, 126, 1), pltpu.roll(found, 2, 1)
        )
        count = found[2:3]
        mean = found[0:1] / count
        var = found[1:2] / count - mean * mean
        scale = lax.rsqrt(var + 1e-6) * gain[...] * 0.5
        shift = bias[...] * 0.5 - mean * scale
        return jnp.broadcast_to(scale, (128, 128)).T, jnp.broadcast_to(shift, (128, 128)).T

    def finish(kept, begin, count, scale_c, shift_c):
        wide = []
        for r in range(count):
            pieces = []
            for i in range(2):
                value = conv[kept, 2 * (begin + r) + i].astype(F32)
                for j in range(2):
                    v = value[:, j * lanes:(j + 1) * lanes] * scale_c + shift_c
                    pieces.append((v + v * jnp.tanh(v)).astype(BF16))
            wide.append(jnp.concatenate(pieces, axis=0))
        result = jnp.dot(
            weights, jnp.concatenate(wide, axis=1), preferred_element_type=F32
        ).astype(BF16)
        for r in range(count):
            for core in range(2):
                latent[kept, core, begin + r] = result[
                    core * 16:core * 16 + 16, r * lanes:(r + 1) * lanes
                ]

    def send_latent(kept, begin, count, frame):
        span = pl.ds(frame * lat_rows + begin, count)
        arrived[span] = latent[kept, c, pl.ds(begin, count)]

        def to(tt, core):
            remote(
                latent.at[kept, core, pl.ds(begin, count)], arrived.at[span],
                lat_send.at[kept], lat_recv.at[0], {"tm": tt, "space": s, "chan": core},
            ).start()

        def others(n):
            step = jnp.where(t < n_tm // 2, n_tm - 1 - n, 1 + n)
            for core in range(2):
                to(lax.rem(t + step, n_tm), core)

        repeat(n_tm - 1, others)
        to(t, 1 - c)

    my_frame = 2 * t + 2 - c

    @pl.when(first)
    def _():
        finish(1, half_index * piece_rows, piece_rows, *moments_of(clip_in[0, 0]))
        send_latent(1, half_index * piece_rows, piece_rows, 0)

    @pl.when(has_main)
    def _():
        found = moments_of(my_clip)
        finish(0, 0, lat_rows, *found)
        send_latent(0, 0, lat_rows, my_frame)

    owner_wait(True)
    owners = pltpu.make_async_copy(meta, ids, local_sem.at[8])
    owners.start()
    owners.wait()

    def slots_of(b):
        taken = jnp.int32(0)
        slots = []
        for n in range(own_rows):
            hit = ids[b, 0, frames_here + n] == t
            slots.append(jnp.where(hit, taken, -1))
            taken = taken + jnp.where(hit, 1, 0)
        return slots

    def place(b, slots):
        for j in range(capacity):
            value = jnp.zeros((16, lanes), BF16)
            for n in range(own_rows):
                value = jnp.where(slots[n] == j, arrived[b * own_rows + n], value)
            out[0, b * capacity + j] = value

    known = [slots_of(b) for b in range(n_tm)] if n_tm <= 4 else None

    def arrived_wait(count):
        span = arrived.at[pl.ds(0, count)]
        remote(
            span, span, lat_send.at[0], lat_recv.at[0], {"tm": t, "space": s, "chan": c}
        ).wait_recv()

    every = n_frames * lat_rows

    @pl.when(first)
    def _():
        arrived_wait(every - lat_rows - piece_rows)

    @pl.when(jnp.logical_and(has_main, t > 0))
    def _():
        arrived_wait(every - lat_rows)

    @pl.when(jnp.logical_not(has_main))
    def _():
        arrived_wait(every)

    if known is None:
        pl.loop(0, n_tm)(lambda b: place(b, slots_of(b)))
    else:
        for b in range(n_tm):
            place(b, known[b])

    peer.wait_send()
    for up, ok in zs:
        @pl.when(ok)
        def _(up=up):
            span = x.at[0, pl.ds(1, rows), 0]
            remote(
                span, span, z_send.at[int(up)], z_recv.at[0],
                {"tm": t, "space": s, "chan": c},
            ).wait_send()
    for low, ok in sides:
        @pl.when(ok)
        def _(low=low):
            there = x.at[pl.ds(0, 2), 0]
            remote(
                there, there, edge_send.at[int(low)], edge_recv.at[int(low)],
                {"tm": t, "space": s, "chan": c},
            ).wait_send()

            @pl.when(gets_z)
            def _():
                forward(low).wait_send()

    @pl.when(meta_sent)
    def _():
        meta_copy.wait_send()

    stat_wait(False)
    owner_wait(False)

    def latents_left(kept, count):
        span = arrived.at[pl.ds(0, count)]
        remote(
            span, span, lat_send.at[kept], lat_recv.at[0], {"tm": t, "space": s, "chan": c}
        ).wait_send()

    @pl.when(first)
    def _():
        latents_left(1, (2 * n_tm - 1) * piece_rows)

    @pl.when(has_main)
    def _():
        latents_left(0, (2 * n_tm - 1) * lat_rows)


def solution(mesh):
    n_tm, n_space = mesh.shape["tm"], mesh.shape["space"]
    total = n_tm * n_space * 2

    def shards(activations, frame_clip, conv_weight, norm_gain, norm_bias, out_weight, owner):
        half, frames_here, rows, columns = activations.shape
        lat_rows = rows // 2
        capacity = max(2, 2 * frames_here * lat_rows // n_tm)
        moments = out_weight.shape[-1]
        dma = pltpu.SemaphoreType.DMA
        return pl.pallas_call(
            functools.partial(kernel, (n_tm, n_space, capacity)),
            out_shape=jax.ShapeDtypeStruct(
                (1, n_tm * capacity, moments // 2, columns // 2), BF16
            ),
            in_specs=[pl.BlockSpec(memory_space=pltpu.HBM)] * 7,
            out_specs=pl.BlockSpec(memory_space=pltpu.VMEM),
            scratch_shapes=[
                pltpu.SMEM((1, frames_here), jnp.int32),
                pltpu.SMEM((1, frames_here * lat_rows), jnp.int32),
                pltpu.VMEM(activations.shape, BF16),
                pltpu.VMEM(conv_weight.shape, BF16),
                pltpu.VMEM((1, CHANNELS), F32),
                pltpu.VMEM((1, CHANNELS), F32),
                pltpu.VMEM((4, moments, CHANNELS), BF16),
                pltpu.VMEM((8, 128), jnp.int32),
                pltpu.VMEM((8, 128), jnp.int32),
                pltpu.SMEM((8, 128), jnp.int32),
                pltpu.VMEM((n_tm, 8, 128), jnp.int32),
                pltpu.VMEM((3, rows + 2, 2, half, columns), BF16),
                pltpu.VMEM((384, 1152), BF16),
                pltpu.VMEM((384, 384), BF16),
                pltpu.VMEM((rows, 384, columns), F32),
                pltpu.VMEM((2, rows, CHANNELS, columns), BF16),
                pltpu.VMEM((8, 128), F32),
                pltpu.VMEM((total, 8, 128), F32),
                pltpu.SMEM((n_tm, 8, 128), jnp.int32),
                pltpu.VMEM((2, 2, lat_rows, moments // 2, columns // 2), BF16),
                pltpu.VMEM((n_tm * frames_here * lat_rows, moments // 2, columns // 2), BF16),
                pltpu.VMEM((2, CHANNELS, columns // 2), F32),
                pltpu.SemaphoreType.REGULAR((2,)),
                dma((2,)),
                dma((3,)),
                dma((2,)),
                dma((2,)),
                dma((2,)),
                dma((2,)),
                dma((1,)),
                dma((1,)),
                dma((2,)),
                dma((2,)),
                dma((1,)),
                dma((1,)),
                dma((1,)),
                dma((1,)),
                dma((2,)),
                dma((1,)),
                dma((9,)),
            ],
            compiler_params=pltpu.CompilerParams(
                collective_id=0, has_side_effects=True, vmem_limit_bytes=24 * 1024 * 1024
            ),
        )(*(
            pltpu.with_memory_space_constraint(operand, pltpu.HBM)
            for operand in (
                frame_clip.reshape(1, -1), owner.reshape(1, -1), activations, conv_weight,
                norm_gain.reshape(1, -1), norm_bias.reshape(1, -1),
                out_weight.transpose(0, 1, 3, 2).reshape(4, moments, CHANNELS),
            )
        ))

    placed = (
        P(("groups", "chan"), "tm", "space", None),
        P(("groups", "tm")),
        P(),
        P(),
        P(),
        P(),
        P(("groups", "space"), "tm", None),
    )
    return jax.shard_map(
        shards,
        mesh=mesh,
        in_specs=placed,
        out_specs=P(("groups", "space"), "tm", "chan", None),
        check_vma=False,
    )
```
